256 devices in a mesh: ctx: 32 (over y, z), head: 8 (over x, core).
Axes of the slice: x: 4, y: 4, z: 8, core: 2. Of those that a mesh axis runs over, the one named last changes fastest.
Arguments:
- queries: bfloat16 [4096, 64, 576], P('ctx', 'head'), may hold values from -16 to 16
- latents: bfloat16 [131072, 576], P('ctx'), may hold values from -6 to 6
- selected: int32 [64, 32], P('ctx'), may hold values from 0 to 2047, as said below
- w_uv: bfloat16 [64, 512, 128], P('head'), may hold values from -3 to 3
- w_out: bfloat16 [8192, 4096], P('head', 'ctx'), may hold values from -0.0625 to 0.0625
Outputs:
- mixed: bfloat16 [4096, 4096], P('ctx', 'head')
The draws below stay inside these ranges and needn't reach their ends.
Inputs may be any that keep to these rules, and one draw needn't show every extreme that they name: `selected`: row g lists 32 different key blocks, none after the block at the position of query block g; that block and block 0 are always among them. At most 2 blocks of a row lie among the 64 blocks of one index of ctx, and the first 64 blocks hold exactly 2 of every row.
All inputs are finite; a program needn't handle non-finite values.
Results may differ from the reference program's by a relative error of at most 0.019.
Values may be sent and summed in bfloat16 or wider, within the bound.
No kernel may reach another device: no remote copies, remote signals or barrier semaphores. Data moves between devices by JAX's collectives and lax.ppermute only.
A program may use at most 128 MiB of HBM per device.

```python
import jax
import jax.numpy as jnp
from jax import lax

LATENT = 512
ROPE = 64
VHEAD = 128
HEADS = 64
OUT_COLS = 4096
BLOCK = 64
SEL = 32
KV_LEN = 131072
QTOK = 4096
NBLK = 2048
QBLOCKS = 64
NB_DEV = 64
PER_OWNER = 2
N_CTX = 32


def pick_blocks(key):
    first_key, second_key = jax.random.split(jax.random.fold_in(key, 7), 2)
    pair_count = N_CTX * PER_OWNER
    block_pos = (KV_LEN - QTOK) // BLOCK + jnp.arange(QBLOCKS, dtype=jnp.int32)
    pair_ids = jnp.arange(pair_count, dtype=jnp.int32)
    owners = pair_ids // PER_OWNER
    ranks = pair_ids % PER_OWNER
    avail = jnp.clip(block_pos[:, None] - owners[None, :] * NB_DEV + 1, 0, NB_DEV)
    usable = ranks[None, :] < avail
    own_pos = block_pos // NB_DEV
    forced = (owners[None, :] == 0) | (owners[None, :] == own_pos[:, None]) & (ranks[None, :] == 0)
    recent = owners[None, :] >= own_pos[:, None] - 1
    base = jax.random.randint(first_key, (QBLOCKS, pair_count), 0, 65536)
    score = jnp.where(usable, base + jnp.where(recent, 65536, 0), -1048576)
    score = jnp.where(forced, 1048576, score)
    score = score * 128 + pair_ids[None, :]
    unused, chosen = lax.top_k(score, SEL)
    chosen_owner = chosen // PER_OWNER
    chosen_rank = chosen % PER_OWNER
    chosen_avail = jnp.take_along_axis(avail, chosen, axis=1)
    spread = jnp.maximum(chosen_avail // PER_OWNER, 1)
    offset = jax.random.randint(second_key, (QBLOCKS, SEL), 0, 1048576) % spread
    offset = jnp.where((chosen_owner == 0) & (chosen_rank == PER_OWNER - 1), spread - 1, offset)
    offset = jnp.where((chosen_owner == own_pos[:, None]) & (chosen_rank == 0), 0, offset)
    local = chosen_avail - 1 - (chosen_rank * spread + offset)
    return (chosen_owner * NB_DEV + local).astype(jnp.int32)


def draw_selected(key, part):
    return pick_blocks(key)


def draw_queries(key, part):
    shape = (QTOK, HEADS, LATENT + ROPE)
    inner = jax.random.fold_in(key, 11)
    values = jnp.clip(jax.random.normal(inner, shape, jnp.float32), -6.0, 6.0)
    return values.astype(jnp.bfloat16)


def draw_latents(key, part):
    shape = (KV_LEN, LATENT + ROPE)
    inner = jax.random.fold_in(key, 13)
    values = jnp.clip(jax.random.normal(inner, shape, jnp.float32), -6.0, 6.0)
    return values.astype(jnp.bfloat16)


def block_scale(own_key, extent, shards, smallest, top_value):
    gain, own = 1.0, jax.random.fold_in(own_key, 6)
    for dim, blocks in shards:
        heights = jnp.exp(jax.random.uniform(jax.random.fold_in(own, dim), (blocks,), jnp.float32, smallest / len(shards), top_value / len(shards)))
        gain = gain * jnp.repeat(heights, extent[dim] // blocks).reshape([-1 if axis == dim else 1 for axis in range(len(extent))])
    return gain


def normal_values(stream_key, shape, scale, limit, shards=(), held_as=jnp.bfloat16):
    array = jax.random.normal(stream_key, shape, jnp.float32) * scale
    if len(shards) > 0:
        array = block_scale(stream_key, shape, shards, -0.22, 0.18) * array
    return jnp.clip(array, min=-limit, max=limit).astype(held_as)


def setup_inputs(seed: int = 0) -> dict:
    arg_keys = jax.random.split(jax.random.key(seed), 6)
    queries = draw_queries(jax.random.fold_in(arg_keys[5], 71), 0)
    latents = draw_latents(jax.random.fold_in(arg_keys[5], 71), 0)
    selected = draw_selected(jax.random.fold_in(arg_keys[5], 71), 0)
    w_uv = normal_values(arg_keys[3], (HEADS, LATENT, VHEAD), 4 ** -0.5, 3.0, ((0, 8),))
    w_out = normal_values(arg_keys[4], (HEADS * VHEAD, OUT_COLS), (HEADS * VHEAD) ** -0.5, 0.0625, ((0, 8), (1, 32)))
    return dict(queries=queries, latents=latents, selected=selected, w_uv=w_uv, w_out=w_out)


SCALE = 192.0 ** -0.5


def attend_block(query_rows, keys, key_blocks, first_pos):
    heads_here = query_rows.shape[1]
    width = query_rows.shape[2]
    flat_keys = keys.reshape(-1, width)
    scores = lax.dot_general(query_rows.reshape(-1, width), flat_keys, (((1,), (1,)), ((), ())), preferred_element_type=jnp.float32) * SCALE
    key_pos = (key_blocks[:, None] * BLOCK + jnp.arange(BLOCK, dtype=jnp.int32)[None, :]).reshape(-1)
    query_pos = first_pos + jnp.arange(BLOCK * heads_here, dtype=jnp.int32) // heads_here
    scores = jnp.where(key_pos[None, :] <= query_pos[:, None], scores, -jnp.inf)
    peak = jnp.max(scores, axis=1, keepdims=True)
    expo = jnp.exp(scores - peak)
    probs = (expo / jnp.sum(expo, axis=1, keepdims=True)).astype(jnp.bfloat16)
    attended = jnp.dot(probs, flat_keys[:, :LATENT], preferred_element_type=jnp.float32).astype(jnp.bfloat16)
    return attended.reshape(BLOCK, heads_here, LATENT)


def reference(queries, latents, selected, w_uv, w_out):
    width = LATENT + ROPE
    first_row = KV_LEN - QTOK
    block_keys = latents.reshape(NBLK, BLOCK, width)

    def one_block(inputs):
        rows, picks, index = inputs
        keys = jnp.take(block_keys, picks, axis=0)
        return attend_block(rows, keys, picks, first_row + index * BLOCK)

    attended = lax.map(one_block, (queries.reshape(QBLOCKS, BLOCK, HEADS, width), selected, jnp.arange(QBLOCKS, dtype=jnp.int32)))
    attended = attended.reshape(QTOK, HEADS, LATENT)
    head_values = jnp.einsum("thl,hlv->thv", attended.astype(jnp.float32), w_uv.astype(jnp.float32)).astype(jnp.bfloat16)
    return jnp.dot(head_values.reshape(QTOK, HEADS * VHEAD), w_out, preferred_element_type=jnp.float32).astype(jnp.bfloat16)
```

```python
import functools

import jax
import jax.numpy as jnp
from jax import lax
from jax.experimental import pallas as pl
from jax.experimental.pallas import tpu as pltpu
from jax.sharding import PartitionSpec as P

LATENT = 512
ROPE = 64
WIDTH = LATENT + ROPE
PAIR = 2 * WIDTH
VHEAD = 128
BLOCK = 64
SEL = 32
PER_OWNER = 2
XDIM = 4
SUB = BLOCK // XDIM
SCALE = 192.0 ** (-0.5)
LOG2E = 1.4426950408889634


def gather_kernel(req_ref, x_ref, lat_ref, out_ref, buf, sem):
    n_req = out_ref.shape[0]
    start = x_ref[0] * SUB

    def issue(i, carry):
        row = pl.multiple_of(req_ref[i] * BLOCK + start, SUB)
        pltpu.make_async_copy(lat_ref.at[pl.ds(row, SUB), :], buf.at[i], sem).start()
        return carry

    lax.fori_loop(0, 2 * n_req, issue, 0)
    pltpu.make_async_copy(buf, buf, sem).wait()

    def pack(r, carry):
        first = buf[2 * r]
        second = buf[2 * r + 1]
        out_ref[r, :, :LATENT] = first[:, :LATENT]
        out_ref[r, :, LATENT : 2 * LATENT] = second[:, :LATENT]
        out_ref[r, :, 2 * LATENT :] = jnp.concatenate([first[:, LATENT:], second[:, LATENT:]], axis=1)
        return carry

    lax.fori_loop(0, n_req, pack, 0)


def gather_rows(req, x, latents, n_ctx):
    return pl.pallas_call(
        gather_kernel,
        out_shape=jax.ShapeDtypeStruct((n_ctx, SUB, PAIR), jnp.bfloat16),
        in_specs=[
            pl.BlockSpec(memory_space=pltpu.SMEM),
            pl.BlockSpec(memory_space=pltpu.SMEM),
            pl.BlockSpec(memory_space=pl.ANY),
        ],
        out_specs=pl.BlockSpec(memory_space=pltpu.VMEM),
        scratch_shapes=[
            pltpu.VMEM((n_ctx * PER_OWNER, SUB, WIDTH), jnp.bfloat16),
            pltpu.SemaphoreType.DMA(()),
        ],
        compiler_params=pltpu.CompilerParams(vmem_limit_bytes=16 * 2**20),
        cost_estimate=pl.CostEstimate(flops=0, bytes_accessed=4 * 2**20, transcendentals=0),
        name="gather_rows",
    )(req, x, latents)


def compact_kernel(owner_ref, rank_ref, recv_ref, out_ref):
    def pair(p, carry):
        half = lax.broadcasted_iota(jnp.int32, (SUB, 2 * ROPE), 1) // ROPE
        ropes = []
        for side in range(2):
            owner = owner_ref[2 * p + side]
            rank = rank_ref[2 * p + side]
            lane = pl.multiple_of(rank * LATENT, LATENT)
            out_ref[p, :, side * LATENT : (side + 1) * LATENT] = recv_ref[owner, :, pl.ds(lane, LATENT)]
            tail = recv_ref[owner, :, 2 * LATENT :].astype(jnp.float32)
            ropes.append(jnp.where(rank == side, tail, pltpu.roll(tail, ROPE, 1)))
        out_ref[p, :, 2 * LATENT :] = jnp.where(half == 0, ropes[0], ropes[1]).astype(jnp.bfloat16)
        return carry

    lax.fori_loop(0, out_ref.shape[0], pair, 0)


def compact(owner, rank, recv):
    return pl.pallas_call(
        compact_kernel,
        out_shape=jax.ShapeDtypeStruct((SEL // 2, SUB, PAIR), jnp.bfloat16),
        in_specs=[
            pl.BlockSpec(memory_space=pltpu.SMEM),
            pl.BlockSpec(memory_space=pltpu.SMEM),
            pl.BlockSpec(memory_space=pltpu.VMEM),
        ],
        out_specs=pl.BlockSpec(memory_space=pltpu.VMEM),
        compiler_params=pltpu.CompilerParams(vmem_limit_bytes=16 * 2**20),
        cost_estimate=pl.CostEstimate(flops=0, bytes_accessed=2 * 2**20, transcendentals=0),
        name="compact",
    )(owner, rank, recv)


def attend_kernel(first_ref, pos_ref, qa_ref, qb_ref, k0, k1, k2, k3, w_ref, out_ref):
    rows = qa_ref.shape[0]
    tok = lax.broadcasted_iota(jnp.int32, (rows, 1), 0) % BLOCK
    query_pos = first_ref[0] + tok
    sides = []
    scores = []
    for n, ref in enumerate((k0, k1, k2, k3)):
        tail = ref[:, 2 * LATENT :]
        for side in range(2):
            lat = ref[:, side * LATENT : (side + 1) * LATENT]
            keys = jnp.concatenate([lat, tail], axis=1)
            q = (qa_ref, qb_ref)[side][...]
            s = lax.dot_general(q, keys, (((1,), (1,)), ((), ())), preferred_element_type=jnp.float32)
            col = (2 * n + side) * s.shape[1]
            key_pos = pos_ref[:, col : col + s.shape[1]]
            scores.append(jnp.where(key_pos <= query_pos, s, -jnp.inf))
            sides.append(lat)
    peak = functools.reduce(jnp.maximum, scores)
    peak = jnp.max(peak, axis=1, keepdims=True)
    total = jnp.zeros((rows, scores[0].shape[1]), jnp.float32)
    acc = jnp.zeros((rows, LATENT), jnp.float32)
    for s, lat in zip(scores, sides):
        p = jnp.exp2((s - peak) * (SCALE * LOG2E))
        total = total + p
        acc = acc + jnp.dot(p.astype(jnp.bfloat16), lat, preferred_element_type=jnp.float32)
    attended = (acc / jnp.sum(total, axis=1, keepdims=True)).astype(jnp.bfloat16)
    for n in range(rows // BLOCK):
        values = jnp.dot(attended[n * BLOCK : (n + 1) * BLOCK], w_ref[n], preferred_element_type=jnp.float32)
        out_ref[:, n * VHEAD : (n + 1) * VHEAD] = values.astype(jnp.bfloat16)


def attend(first, pos, qa, qb, chunks, w_uv):
    rows_all = qa.shape[0]
    tile = 256
    heads = tile // BLOCK
    whole = pl.BlockSpec((chunks[0].shape[0], PAIR), lambda i: (0, 0))
    q_spec = pl.BlockSpec((tile, qa.shape[1]), lambda i: (i, 0))
    return pl.pallas_call(
        attend_kernel,
        grid=(rows_all // tile,),
        out_shape=jax.ShapeDtypeStruct((BLOCK, rows_all // BLOCK * VHEAD), jnp.bfloat16),
        in_specs=[
            pl.BlockSpec(memory_space=pltpu.SMEM),
            pl.BlockSpec(pos.shape, lambda i: (0, 0)),
            q_spec,
            q_spec,
            whole,
            whole,
            whole,
            whole,
            pl.BlockSpec((heads, LATENT, VHEAD), lambda i: (i, 0, 0)),
        ],
        out_specs=pl.BlockSpec((BLOCK, heads * VHEAD), lambda i: (0, i)),
        compiler_params=pltpu.CompilerParams(vmem_limit_bytes=40 * 2**20),
        cost_estimate=pl.CostEstimate(flops=5 * 10**9, bytes_accessed=8 * 2**20, transcendentals=2**21),
        name="attend",
    )(first, pos, qa, qb, *chunks, w_uv)


def head_perm(n, offset):
    return [(i, (i + offset) % n) for i in range(n)]


def per_device(queries, latents, selected, w_uv, w_out):
    n_ctx = lax.axis_size("ctx")
    n_head = lax.axis_size("head")
    shard = lax.axis_index("ctx")
    head = lax.axis_index("head")
    core = head % 2
    x = head // 2
    tok_dev, heads_here, width = queries.shape
    blocks_dev = latents.shape[0] // BLOCK
    first_block = blocks_dev * n_ctx - (tok_dev // BLOCK) * n_ctx
    swap = [(i, i ^ 1) for i in range(n_head)]

    picks = jnp.where(core == 0, selected[0], selected[1])
    owner = picks // blocks_dev
    local = picks % blocks_dev
    order = jnp.arange(SEL, dtype=jnp.int32)
    same = (owner[:, None] == owner[None, :]) & (order[None, :] < order[:, None])
    rank = jnp.sum(same.astype(jnp.int32), axis=1)
    slot = owner * PER_OWNER + rank
    match = slot[:, None] == jnp.arange(n_ctx * PER_OWNER, dtype=jnp.int32)[None, :]
    wanted = jnp.sum(jnp.where(match, local[:, None], 0), axis=0).reshape(n_ctx, PER_OWNER)
    req = lax.all_to_all(wanted, "ctx", split_axis=0, concat_axis=0, tiled=True)

    w_all = lax.all_gather(w_out, "ctx", axis=1, tiled=True)

    piece = gather_rows(req.reshape(-1), x.reshape(1), latents, n_ctx)
    recv = lax.all_to_all(piece, "ctx", split_axis=0, concat_axis=0, tiled=True)

    by_block = queries.reshape(2, BLOCK, heads_here, width)
    mine = jnp.where(core == 0, by_block[0], by_block[1])
    theirs = jnp.where(core == 0, by_block[1], by_block[0])
    got = lax.ppermute(theirs, "head", swap)
    w_other = lax.ppermute(w_uv, "head", swap)
    q = jnp.concatenate([mine, got], axis=1).transpose(1, 0, 2).reshape(2 * heads_here * BLOCK, width)
    gap = jnp.zeros((q.shape[0], ROPE), q.dtype)
    qa = jnp.concatenate([q, gap], axis=1)
    qb = jnp.concatenate([q[:, :LATENT], gap, q[:, LATENT:]], axis=1)
    w_pair = jnp.concatenate([w_uv, w_other], axis=0)

    chunk = compact(owner, rank, recv).reshape(SEL // 2 * SUB, PAIR)
    chunks = [chunk] + [lax.ppermute(chunk, "head", head_perm(n_head, 2 * d)) for d in range(1, XDIM)]
    sides = picks.reshape(SEL // 2, 2).T[None, :, :, None] * BLOCK
    part = ((x - jnp.arange(XDIM, dtype=jnp.int32)) % XDIM)[:, None, None, None] * SUB
    pos = (sides + part + jnp.arange(SUB, dtype=jnp.int32)[None, None, None, :]).reshape(1, -1)
    first = (first_block + shard * (tok_dev // BLOCK) + core) * BLOCK
    values = attend(first.reshape(1), pos, qa, qb, chunks, w_pair)

    half = heads_here * VHEAD
    own = values[:, :half]
    other = lax.ppermute(values[:, half:], "head", swap)
    rows = jnp.where(core == 0, jnp.concatenate([own, other]), jnp.concatenate([other, own]))
    partial_rows = jnp.dot(rows, w_all, preferred_element_type=jnp.float32).astype(jnp.bfloat16)
    split = partial_rows.reshape(tok_dev, n_head, -1).transpose(1, 0, 2)
    parts = lax.all_to_all(split, "head", split_axis=0, concat_axis=0, tiled=True)
    return jnp.sum(parts.astype(jnp.float32), axis=0).astype(jnp.bfloat16)


def solution(mesh):
    return jax.shard_map(
        per_device,
        mesh=mesh,
        in_specs=(
            P("ctx", "head", None),
            P("ctx", None),
            P("ctx", None),
            P("head", None, None),
            P("head", "ctx"),
        ),
        out_specs=P("ctx", "head"),
        check_vma=False,
    )
```

```python
import functools

import jax
import jax.numpy as jnp
from jax import lax
from jax.experimental import pallas as pl
from jax.experimental.pallas import tpu as pltpu
from jax.sharding import PartitionSpec as P

LATENT = 512
ROPE = 64
WIDTH = LATENT + ROPE
VHEAD = 128
BLOCK = 64
SEL = 32
KEYS = SEL * BLOCK
PER_OWNER = 2
XDIM = 4
YDIM = 4
ZDIM = 8
FEAT = WIDTH // XDIM
LANES = 2 * BLOCK
SCALE = 192.0 ** (-0.5)
LOG2E = 1.4426950408889634


def join_halves(a, a_half, b, b_half):
    low = jnp.where(a_half == 0, a[:, :BLOCK], a[:, BLOCK:])
    high = jnp.where(b_half == 0, b[:, :BLOCK], b[:, BLOCK:])
    return jnp.concatenate([low, high], axis=1)


def gather_kernel(req_ref, x_ref, lat_ref, out_ref, buf, sem):
    n_req = out_ref.shape[0]
    feat = pl.multiple_of(x_ref[0] * FEAT, 16)

    def block_of(i, side):
        return req_ref[i] // BLOCK if side == 0 else req_ref[i] % BLOCK

    def issue(i, carry):
        for side in range(2):
            col = pl.multiple_of(block_of(i, side) // 2 * LANES, LANES)
            pltpu.make_async_copy(
                lat_ref.at[pl.ds(feat, FEAT), pl.ds(col, LANES)], buf.at[2 * i + side], sem
            ).start()
        return carry

    lax.fori_loop(0, n_req, issue, 0)
    pltpu.make_async_copy(buf, buf, sem).wait()

    def pack(i, carry):
        out_ref[i] = join_halves(buf[2 * i], block_of(i, 0) % 2, buf[2 * i + 1], block_of(i, 1) % 2)
        return carry

    lax.fori_loop(0, n_req, pack, 0)


def gather_rows(req, x, latents_t, n_ctx):
    return pl.pallas_call(
        gather_kernel,
        out_shape=jax.ShapeDtypeStruct((n_ctx, FEAT, LANES), jnp.bfloat16),
        in_specs=[
            pl.BlockSpec(memory_space=pltpu.SMEM),
            pl.BlockSpec(memory_space=pltpu.SMEM),
            pl.BlockSpec(memory_space=pl.ANY),
        ],
        out_specs=pl.BlockSpec(memory_space=pltpu.VMEM),
        scratch_shapes=[
            pltpu.VMEM((n_ctx * PER_OWNER, FEAT, LANES), jnp.bfloat16),
            pltpu.SemaphoreType.DMA(()),
        ],
        compiler_params=pltpu.CompilerParams(vmem_limit_bytes=60 * 2**20),
        cost_estimate=pl.CostEstimate(flops=0, bytes_accessed=4 * 2**20, transcendentals=0),
        name="gather_rows",
    )(req, x, latents_t)


def compact_kernel(owner_ref, rank_ref, recv_ref, out_ref):
    for p in range(SEL // 2):
        a, b = 2 * p, 2 * p + 1
        out_ref[:, p * LANES : (p + 1) * LANES] = join_halves(
            recv_ref[owner_ref[a]], rank_ref[a], recv_ref[owner_ref[b]], rank_ref[b]
        )


def compact(owner, rank, recv):
    return pl.pallas_call(
        compact_kernel,
        out_shape=jax.ShapeDtypeStruct((FEAT, KEYS), jnp.bfloat16),
        in_specs=[
            pl.BlockSpec(memory_space=pltpu.SMEM),
            pl.BlockSpec(memory_space=pltpu.SMEM),
            pl.BlockSpec(memory_space=pltpu.VMEM),
        ],
        out_specs=pl.BlockSpec(memory_space=pltpu.VMEM),
        compiler_params=pltpu.CompilerParams(vmem_limit_bytes=16 * 2**20),
        cost_estimate=pl.CostEstimate(flops=0, bytes_accessed=2 * 2**20, transcendentals=0),
        name="compact",
    )(owner, rank, recv)


def attend_kernel(info_ref, pos_ref, q_ref, k0, k1, k2, k3, w_ref, out_ref, keys):
    rows = q_ref.shape[0]

    @pl.when(pl.program_id(0) == 0)
    def _():
        for n, ref in enumerate((k0, k1, k2, k3)):
            part = lax.rem(info_ref[1] + XDIM - n, XDIM)
            keys[pl.ds(pl.multiple_of(part * FEAT, 16), FEAT), :] = ref[...]

    tok = lax.broadcasted_iota(jnp.int32, (rows, 1), 0) % BLOCK
    query_pos = info_ref[0] + tok
    q = q_ref[...]
    width = 512
    scores = []
    for c in range(0, KEYS, width):
        s = jnp.dot(q, keys[:, c : c + width], preferred_element_type=jnp.float32)
        scores.append(jnp.where(pos_ref[:, c : c + width] <= query_pos, s, -jnp.inf))
    peak = jnp.max(functools.reduce(jnp.maximum, scores), axis=1, keepdims=True)
    total = jnp.zeros((rows, width), jnp.float32)
    acc = jnp.zeros((rows, LATENT), jnp.float32)
    for n, s in enumerate(scores):
        p = jnp.exp2((s - peak) * (SCALE * LOG2E))
        total = total + p
        acc = acc + lax.dot_general(
            p.astype(jnp.bfloat16),
            keys[:LATENT, n * width : (n + 1) * width],
            (((1,), (1,)), ((), ())),
            preferred_element_type=jnp.float32,
        )
    attended = (acc / jnp.sum(total, axis=1, keepdims=True)).astype(jnp.bfloat16)
    for n in range(rows // BLOCK):
        values = jnp.dot(attended[n * BLOCK : (n + 1) * BLOCK], w_ref[n], preferred_element_type=jnp.float32)
        out_ref[:, n * VHEAD : (n + 1) * VHEAD] = values.astype(jnp.bfloat16)


def attend(info, pos, q, chunks, w_uv):
    rows_all = q.shape[0]
    tile = 256
    heads = tile // BLOCK
    whole = pl.BlockSpec((FEAT, KEYS), lambda i: (0, 0))
    return pl.pallas_call(
        attend_kernel,
        grid=(rows_all // tile,),
        out_shape=jax.ShapeDtypeStruct((BLOCK, rows_all // BLOCK * VHEAD), jnp.bfloat16),
        in_specs=[
            pl.BlockSpec(memory_space=pltpu.SMEM),
            pl.BlockSpec(pos.shape, lambda i: (0, 0)),
            pl.BlockSpec((tile, WIDTH), lambda i: (i, 0)),
            whole,
            whole,
            whole,
            whole,
            pl.BlockSpec((heads, LATENT, VHEAD), lambda i: (i, 0, 0)),
        ],
        out_specs=pl.BlockSpec((BLOCK, heads * VHEAD), lambda i: (0, i)),
        scratch_shapes=[pltpu.VMEM((WIDTH, KEYS), jnp.bfloat16)],
        compiler_params=pltpu.CompilerParams(vmem_limit_bytes=24 * 2**20),
        cost_estimate=pl.CostEstimate(flops=5 * 10**9, bytes_accessed=8 * 2**20, transcendentals=2**21),
        name="attend",
    )(info, pos, q, *chunks, w_uv)


def project_kernel(info_ref, h0, h1, h2, h3, w_own, w_other, out_ref, rows):
    @pl.when(pl.program_id(0) == 0)
    def _():
        for n, ref in enumerate((h0, h1, h2, h3)):
            slot = lax.rem(info_ref[0] + YDIM - n, YDIM)
            rows[pl.ds(pl.multiple_of(slot * BLOCK, BLOCK), BLOCK), :] = ref[...]

    depth = w_own.shape[0]
    out = jnp.dot(rows[:, :depth], w_own[...], preferred_element_type=jnp.float32)
    out = out + jnp.dot(rows[:, depth:], w_other[...], preferred_element_type=jnp.float32)
    out_ref[0] = out.astype(jnp.bfloat16)


def project(info, pieces, w_own, w_other):
    depth, cols = w_own.shape
    tile = 256
    per_half = cols // 2 // tile
    piece = pl.BlockSpec(pieces[0].shape, lambda i, info: (0, 0))
    w_spec = pl.BlockSpec((depth, tile), lambda i, info: (0, i))
    return pl.pallas_call(
        project_kernel,
        grid_spec=pltpu.PrefetchScalarGridSpec(
            num_scalar_prefetch=1,
            grid=(cols // tile,),
            in_specs=[piece] * 4 + [w_spec, w_spec],
            out_specs=pl.BlockSpec(
                (1, YDIM * BLOCK, tile),
                lambda i, info: (lax.rem(i // per_half + info[1], 2), 0, lax.rem(i, per_half)),
            ),
            scratch_shapes=[pltpu.VMEM((YDIM * BLOCK, pieces[0].shape[1]), jnp.bfloat16)],
        ),
        out_shape=jax.ShapeDtypeStruct((2, YDIM * BLOCK, cols // 2), jnp.bfloat16),
        compiler_params=pltpu.CompilerParams(vmem_limit_bytes=24 * 2**20),
        cost_estimate=pl.CostEstimate(flops=10**9, bytes_accessed=6 * 2**20, transcendentals=0),
        name="project",
    )(info, *pieces, w_own, w_other)


def per_device(queries, latents, selected, w_uv, w_out):
    n_ctx = lax.axis_size("ctx")
    n_head = lax.axis_size("head")
    shard = lax.axis_index("ctx")
    head = lax.axis_index("head")
    core = jnp.bitwise_and(head, 1)
    x = lax.shift_right_logical(head, 1)
    y = lax.shift_right_logical(shard, 3)
    tok_dev, heads_here, width = queries.shape
    blocks_dev = latents.shape[0] // BLOCK
    first_block = blocks_dev * n_ctx - (tok_dev // BLOCK) * n_ctx
    swap = [(i, i ^ 1) for i in range(n_head)]

    picks = jnp.where(core == 0, selected[0], selected[1])
    owner = lax.shift_right_logical(picks, 6)
    local = jnp.bitwise_and(picks, blocks_dev - 1)
    order = jnp.arange(SEL, dtype=jnp.int32)
    same = (owner[:, None] == owner[None, :]) & (order[None, :] < order[:, None])
    rank = jnp.sum(same.astype(jnp.int32), axis=1)
    code = jnp.where(rank == 0, local * BLOCK, local)
    match = owner[:, None] == jnp.arange(n_ctx, dtype=jnp.int32)[None, :]
    wanted = jnp.sum(jnp.where(match, code[:, None], 0), axis=0)
    req = lax.all_to_all(wanted, "ctx", split_axis=0, concat_axis=0, tiled=True)

    groups = [[g * ZDIM + z for z in range(ZDIM)] for g in range(YDIM)]
    w_own = lax.all_gather(w_out, "ctx", axis=1, tiled=True, axis_index_groups=groups)
    w_other = lax.ppermute(w_own, "head", swap)

    piece = gather_rows(req.reshape(-1), x.reshape(1), latents.T, n_ctx)
    recv = lax.all_to_all(piece, "ctx", split_axis=0, concat_axis=0, tiled=True)

    by_head = queries.transpose(1, 0, 2)
    mine = lax.dynamic_slice_in_dim(by_head, core * BLOCK, BLOCK, axis=1)
    theirs = lax.dynamic_slice_in_dim(by_head, (1 - core) * BLOCK, BLOCK, axis=1)
    got = lax.ppermute(theirs, "head", swap)
    uv_other = lax.ppermute(w_uv, "head", swap)
    q = jnp.concatenate([mine, got], axis=0).reshape(2 * heads_here * BLOCK, width)
    uv_pair = jnp.concatenate([w_uv, uv_other], axis=0)

    chunk = compact(owner, rank, recv)
    chunks = [chunk]
    for d in range(1, XDIM):
        chunks.append(lax.ppermute(chunk, "head", [(i, (i + 2 * d) % n_head) for i in range(n_head)]))
    pos = (picks[:, None] * BLOCK + jnp.arange(BLOCK, dtype=jnp.int32)[None, :]).reshape(1, -1)
    first = (first_block + shard * (tok_dev // BLOCK) + core) * BLOCK
    values = attend(jnp.stack([first, x]), pos, q, chunks, uv_pair)

    pieces = [values]
    for d in range(1, YDIM):
        pieces.append(lax.ppermute(values, "ctx", [(i, (i + ZDIM * d) % n_ctx) for i in range(n_ctx)]))
    partial_rows = project(jnp.stack([(y - x) % YDIM, core]), pieces, w_own, w_other)
    other = lax.ppermute(partial_rows[1], "head", swap)
    both = jnp.concatenate(
        [partial_rows[0].reshape(YDIM, BLOCK, -1), other.reshape(YDIM, BLOCK, -1)], axis=1
    )
    total = jnp.zeros(both.shape[1:], jnp.float32)
    for r in range(YDIM):
        route = []
        for c in range(n_ctx):
            for h in range(n_head):
                to = ((h // 2 + r) % YDIM * ZDIM + c % ZDIM) * n_head + c // ZDIM * 2 + h % 2
                route.append((c * n_head + h, to))
        total = total + lax.ppermute(both[r], ("ctx", "head"), route).astype(jnp.float32)
    total = total.astype(jnp.bfloat16)
    return jnp.where(core == 0, total, jnp.concatenate([total[BLOCK:], total[:BLOCK]], axis=0))


def solution(mesh):
    return jax.shard_map(
        per_device,
        mesh=mesh,
        in_specs=(
            P("ctx", "head", None),
            P("ctx", None),
            P("ctx", None),
            P("head", None, None),
            P("head", "ctx"),
        ),
        out_specs=P("ctx", "head"),
        check_vma=False,
    )
```

```python
import functools

import jax
import jax.numpy as jnp
from jax import lax
from jax.experimental import pallas as pl
from jax.experimental.pallas import tpu as pltpu
from jax.sharding import PartitionSpec as P

LATENT = 512
ROPE = 64
WIDTH = LATENT + ROPE
VHEAD = 128
BLOCK = 64
SEL = 32
KEYS = SEL * BLOCK
PER_OWNER = 2
XDIM = 4
YDIM = 4
ZDIM = 8
FEAT = WIDTH // XDIM
LANES = 2 * BLOCK
SCALE = 192.0 ** (-0.5)
LOG2E = 1.4426950408889634


def join_halves(a, a_half, b, b_half):
    low = jnp.where(a_half == 0, a[:, :BLOCK], a[:, BLOCK:])
    high = jnp.where(b_half == 0, b[:, :BLOCK], b[:, BLOCK:])
    return jnp.concatenate([low, high], axis=1)


def gather_kernel(req_ref, slab_ref, out_ref):
    def pack(i, carry):
        pieces = []
        for side in range(2):
            block = req_ref[2 * i + side]
            col = pl.multiple_of(lax.shift_right_logical(block, 1) * LANES, LANES)
            pieces += [slab_ref[:, pl.ds(col, LANES)], jnp.bitwise_and(block, 1)]
        out_ref[i] = join_halves(*pieces)
        return carry

    lax.fori_loop(0, out_ref.shape[0], pack, 0, unroll=4)


def gather_rows(req, slab, n_ctx):
    return pl.pallas_call(
        gather_kernel,
        out_shape=jax.ShapeDtypeStruct((n_ctx, FEAT, LANES), jnp.bfloat16),
        in_specs=[
            pl.BlockSpec(memory_space=pltpu.SMEM),
            pl.BlockSpec(memory_space=pltpu.VMEM),
        ],
        out_specs=pl.BlockSpec(memory_space=pltpu.VMEM),
        compiler_params=pltpu.CompilerParams(vmem_limit_bytes=16 * 2**20),
        cost_estimate=pl.CostEstimate(flops=0, bytes_accessed=4 * 2**20, transcendentals=0),
        name="gather_rows",
    )(req, slab)


def compact_kernel(owner_ref, rank_ref, recv_ref, out_ref):
    for p in range(SEL // 2):
        a, b = 2 * p, 2 * p + 1
        out_ref[:, p * LANES : (p + 1) * LANES] = join_halves(
            recv_ref[owner_ref[a]], rank_ref[a], recv_ref[owner_ref[b]], rank_ref[b]
        )


def compact(owner, rank, recv):
    return pl.pallas_call(
        compact_kernel,
        out_shape=jax.ShapeDtypeStruct((FEAT, KEYS), jnp.bfloat16),
        in_specs=[
            pl.BlockSpec(memory_space=pltpu.SMEM),
            pl.BlockSpec(memory_space=pltpu.SMEM),
            pl.BlockSpec(memory_space=pltpu.VMEM),
        ],
        out_specs=pl.BlockSpec(memory_space=pltpu.VMEM),
        compiler_params=pltpu.CompilerParams(vmem_limit_bytes=16 * 2**20),
        cost_estimate=pl.CostEstimate(flops=0, bytes_accessed=2 * 2**20, transcendentals=0),
        name="compact",
    )(owner, rank, recv)


def attend_kernel(info_ref, pos_ref, q_ref, k0, k1, k2, k3, w_ref, out_ref, keys, sem):
    rows = q_ref.shape[0]

    @pl.when(pl.program_id(0) == 0)
    def _():
        copies = []
        for n, ref in enumerate((k0, k1, k2, k3)):
            part = lax.rem(info_ref[1] + XDIM - n, XDIM)
            place = pl.ds(pl.multiple_of(part * FEAT, 16), FEAT)
            copies.append(pltpu.make_async_copy(ref, keys.at[place, :], sem.at[n]))
        for copy in copies:
            copy.start()
        for copy in copies:
            copy.wait()

    tok = lax.broadcasted_iota(jnp.int32, (rows, 1), 0) % BLOCK
    query_pos = info_ref[0] + tok
    q = q_ref[...]
    width = 512
    scores = []
    for c in range(0, KEYS, width):
        s = jnp.dot(q, keys[:, c : c + width], preferred_element_type=jnp.float32)
        scores.append(jnp.where(pos_ref[:, c : c + width] <= query_pos, s, -jnp.inf))
    peak = jnp.max(functools.reduce(jnp.maximum, scores), axis=1, keepdims=True)
    total = jnp.zeros((rows, width), jnp.float32)
    acc = jnp.zeros((rows, LATENT), jnp.float32)
    for n, s in enumerate(scores):
        p = jnp.exp2((s - peak) * (SCALE * LOG2E))
        total = total + p
        acc = acc + lax.dot_general(
            p.astype(jnp.bfloat16),
            keys[:LATENT, n * width : (n + 1) * width],
            (((1,), (1,)), ((), ())),
            preferred_element_type=jnp.float32,
        )
    attended = (acc / jnp.sum(total, axis=1, keepdims=True)).astype(jnp.bfloat16)
    for n in range(rows // BLOCK):
        values = jnp.dot(attended[n * BLOCK : (n + 1) * BLOCK], w_ref[n], preferred_element_type=jnp.float32)
        out_ref[:, n * VHEAD : (n + 1) * VHEAD] = values.astype(jnp.bfloat16)


def attend(info, pos, q, chunks, w_uv):
    rows_all = q.shape[0]
    tile = 256
    heads = tile // BLOCK
    whole = pl.BlockSpec(memory_space=pl.ANY)
    return pl.pallas_call(
        attend_kernel,
        grid=(rows_all // tile,),
        out_shape=jax.ShapeDtypeStruct((BLOCK, rows_all // BLOCK * VHEAD), jnp.bfloat16),
        in_specs=[
            pl.BlockSpec(memory_space=pltpu.SMEM),
            pl.BlockSpec(pos.shape, lambda i: (0, 0)),
            pl.BlockSpec((tile, WIDTH), lambda i: (i, 0)),
            whole,
            whole,
            whole,
            whole,
            pl.BlockSpec((heads, LATENT, VHEAD), lambda i: (i, 0, 0)),
        ],
        out_specs=pl.BlockSpec((BLOCK, heads * VHEAD), lambda i: (0, i)),
        scratch_shapes=[pltpu.VMEM((WIDTH, KEYS), jnp.bfloat16), pltpu.SemaphoreType.DMA((XDIM,))],
        compiler_params=pltpu.CompilerParams(vmem_limit_bytes=24 * 2**20),
        cost_estimate=pl.CostEstimate(flops=5 * 10**9, bytes_accessed=8 * 2**20, transcendentals=2**21),
        name="attend",
    )(info, pos, q, *chunks, w_uv)


def assemble_kernel(z_ref, *refs):
    shards, out_ref, sem = refs[:ZDIM], refs[ZDIM], refs[ZDIM + 1]
    copies = []
    for n, ref in enumerate(shards):
        col = jnp.bitwise_and(z_ref[0] + n, ZDIM - 1) * VHEAD
        place = pl.ds(pl.multiple_of(col, VHEAD), VHEAD)
        copies.append(pltpu.make_async_copy(ref, out_ref.at[:, place], sem.at[n]))
    for copy in copies:
        copy.start()
    for copy in copies:
        copy.wait()


def assemble(z, shards):
    depth, cols = shards[0].shape
    return pl.pallas_call(
        assemble_kernel,
        out_shape=jax.ShapeDtypeStruct((depth, ZDIM * cols), jnp.bfloat16),
        in_specs=[pl.BlockSpec(memory_space=pltpu.SMEM)] + [pl.BlockSpec(memory_space=pl.ANY)] * ZDIM,
        out_specs=pl.BlockSpec(memory_space=pl.ANY),
        scratch_shapes=[pltpu.SemaphoreType.DMA((ZDIM,))],
        compiler_params=pltpu.CompilerParams(vmem_limit_bytes=8 * 2**20),
        cost_estimate=pl.CostEstimate(flops=0, bytes_accessed=4 * 2**20, transcendentals=0),
        name="assemble",
    )(z, *shards)


def project_kernel(info_ref, h0, h1, h2, h3, w_own, w_other, out_ref, rows):
    @pl.when(pl.program_id(0) == 0)
    def _():
        for n, ref in enumerate((h0, h1, h2, h3)):
            slot = lax.rem(info_ref[0] + YDIM - n, YDIM)
            rows[pl.ds(pl.multiple_of(slot * BLOCK, BLOCK), BLOCK), :] = ref[...]

    depth = w_own.shape[0]
    out = jnp.dot(rows[:, :depth], w_own[...], preferred_element_type=jnp.float32)
    out = out + jnp.dot(rows[:, depth:], w_other[...], preferred_element_type=jnp.float32)
    out_ref[0] = out.astype(jnp.bfloat16)


def project(info, pieces, w_own, w_other):
    depth, cols = w_own.shape
    tile = 256
    per_half = cols // 2 // tile
    piece = pl.BlockSpec(pieces[0].shape, lambda i, info: (0, 0))
    w_spec = pl.BlockSpec((depth, tile), lambda i, info: (0, i))
    return pl.pallas_call(
        project_kernel,
        grid_spec=pltpu.PrefetchScalarGridSpec(
            num_scalar_prefetch=1,
            grid=(cols // tile,),
            in_specs=[piece] * 4 + [w_spec, w_spec],
            out_specs=pl.BlockSpec(
                (1, YDIM * BLOCK, tile),
                lambda i, info: (lax.rem(i // per_half + info[1], 2), 0, lax.rem(i, per_half)),
            ),
            scratch_shapes=[pltpu.VMEM((YDIM * BLOCK, pieces[0].shape[1]), jnp.bfloat16)],
        ),
        out_shape=jax.ShapeDtypeStruct((2, YDIM * BLOCK, cols // 2), jnp.bfloat16),
        compiler_params=pltpu.CompilerParams(vmem_limit_bytes=24 * 2**20),
        cost_estimate=pl.CostEstimate(flops=10**9, bytes_accessed=6 * 2**20, transcendentals=0),
        name="project",
    )(info, *pieces, w_own, w_other)


def per_device(queries, latents, selected, w_uv, w_out):
    n_ctx = lax.axis_size("ctx")
    n_head = lax.axis_size("head")
    shard = lax.axis_index("ctx")
    head = lax.axis_index("head")
    core = jnp.bitwise_and(head, 1)
    x = lax.shift_right_logical(head, 1)
    y = lax.shift_right_logical(shard, 3)
    z = jnp.bitwise_and(shard, ZDIM - 1)
    tok_dev, heads_here, width = queries.shape
    blocks_dev = latents.shape[0] // BLOCK
    first_block = blocks_dev * n_ctx - (tok_dev // BLOCK) * n_ctx
    swap = [(i, i ^ 1) for i in range(n_head)]

    def along_x(value, d):
        return lax.ppermute(value, "head", [(i, (i + 2 * d) % n_head) for i in range(n_head)])

    def along_y(value, d):
        return lax.ppermute(value, "ctx", [(i, (i + ZDIM * d) % n_ctx) for i in range(n_ctx)])

    def along_z(value, d):
        return lax.ppermute(value, "ctx", [(i, i // ZDIM * ZDIM + (i + d) % ZDIM) for i in range(n_ctx)])

    up1, down1 = along_z(w_out, 1), along_z(w_out, -1)

    picks = jnp.where(core == 0, selected[0], selected[1])
    owner = lax.shift_right_logical(picks, 6)
    local = jnp.bitwise_and(picks, blocks_dev - 1)
    order = jnp.arange(SEL, dtype=jnp.int32)
    same = (owner[:, None] == owner[None, :]) & (order[None, :] < order[:, None])
    rank = jnp.sum(same.astype(jnp.int32), axis=1)
    slot = owner * PER_OWNER + rank
    match = slot[:, None, None] == (
        jnp.arange(n_ctx, dtype=jnp.int32)[None, :, None] * PER_OWNER
        + jnp.arange(LANES, dtype=jnp.int32)[None, None, :] // BLOCK
    )
    wanted = jnp.sum(jnp.where(match, local[:, None, None], 0), axis=0).astype(jnp.bfloat16)
    req = lax.all_to_all(wanted, "ctx", split_axis=0, concat_axis=0, tiled=True)
    req, up1, down1 = lax.optimization_barrier((req, up1, down1))
    up2, down2 = along_z(up1, 1), along_z(down1, -1)
    req = req[:, ::BLOCK].astype(jnp.int32).reshape(-1)

    slab = lax.dynamic_slice_in_dim(latents.T, x * FEAT, FEAT, axis=0)
    piece = gather_rows(req, slab, n_ctx)
    recv = lax.all_to_all(piece, "ctx", split_axis=0, concat_axis=0, tiled=True)

    by_head = queries.transpose(1, 0, 2)
    mine = lax.dynamic_slice_in_dim(by_head, core * BLOCK, BLOCK, axis=1)
    theirs = lax.dynamic_slice_in_dim(by_head, (1 - core) * BLOCK, BLOCK, axis=1)
    got = lax.ppermute(theirs, "head", swap)
    uv_other = lax.ppermute(w_uv, "head", swap)
    q = jnp.concatenate([mine, got], axis=0).reshape(2 * heads_here * BLOCK, width)
    uv_pair = jnp.concatenate([w_uv, uv_other], axis=0)

    chunk = compact(owner, rank, recv)
    chunk, up2, down2 = lax.optimization_barrier((chunk, up2, down2))
    up3, down3 = along_z(up2, 1), along_z(down2, -1)
    chunks = [chunk] + [along_x(chunk, d) for d in range(1, XDIM)]
    chunks[3], up3, down3 = lax.optimization_barrier((chunks[3], up3, down3))
    up4 = along_z(up3, 1)
    pos = (picks[:, None] * BLOCK + jnp.arange(BLOCK, dtype=jnp.int32)[None, :]).reshape(1, -1)
    first = (first_block + shard * (tok_dev // BLOCK) + core) * BLOCK
    values = attend(jnp.stack([first, x]), pos, q, chunks, uv_pair)

    pieces = [values] + [along_y(values, d) for d in range(1, YDIM)]
    pieces[1], up4 = lax.optimization_barrier((pieces[1], up4))
    w_own = assemble(z.reshape(1), [w_out, down1, down2, down3, up4, up3, up2, up1])
    w_other = lax.ppermute(w_own, "head", swap)
    partial_rows = project(
        jnp.stack([jnp.bitwise_and(y - x, YDIM - 1), core]), pieces, w_own, w_other
    )
    other = lax.ppermute(partial_rows[1], "head", swap)
    both = jnp.concatenate(
        [partial_rows[0].reshape(YDIM, BLOCK, -1), other.reshape(YDIM, BLOCK, -1)], axis=1
    )
    total = both[0].astype(jnp.float32)
    for d in range(1, XDIM):
        total = total + along_x(both[d], d).astype(jnp.float32)
    total = total.astype(jnp.bfloat16)
    total = jnp.where(core == 0, total, jnp.concatenate([total[BLOCK:], total[:BLOCK]], axis=0))
    route = []
    for c in range(n_ctx):
        for h in range(n_head):
            route.append((c * n_head + h, (h // 2 * ZDIM + c % ZDIM) * n_head + c // ZDIM * 2 + h % 2))
    return lax.ppermute(total, ("ctx", "head"), route)


def solution(mesh):
    return jax.shard_map(
        per_device,
        mesh=mesh,
        in_specs=(
            P("ctx", "head", None),
            P("ctx", None),
            P("ctx", None),
            P("head", None, None),
            P("head", "ctx"),
        ),
        out_specs=P("ctx", "head"),
        check_vma=False,
    )
```

```python
import functools

import jax
import jax.numpy as jnp
from jax import lax
from jax.experimental import pallas as pl
from jax.experimental.pallas import tpu as pltpu
from jax.sharding import PartitionSpec as P

LATENT = 512
ROPE = 64
WIDTH = LATENT + ROPE
VHEAD = 128
BLOCK = 64
SEL = 32
KEYS = SEL * BLOCK
PER_OWNER = 2
XDIM = 4
YDIM = 4
ZDIM = 8
FEAT = WIDTH // XDIM
LANES = 2 * BLOCK
SCALE = 192.0 ** (-0.5)
LOG2E = 1.4426950408889634


def join_halves(a, a_half, b, b_half):
    low = jnp.where(a_half == 0, a[:, :BLOCK], a[:, BLOCK:])
    high = jnp.where(b_half == 0, b[:, :BLOCK], b[:, BLOCK:])
    return jnp.concatenate([low, high], axis=1)


def gather_kernel(req_ref, slab_ref, out_ref):
    def pack(i, carry):
        pieces = []
        for side in range(2):
            block = req_ref[2 * i + side]
            col = pl.multiple_of(lax.shift_right_logical(block, 1) * LANES, LANES)
            pieces += [slab_ref[:, pl.ds(col, LANES)], jnp.bitwise_and(block, 1)]
        out_ref[i] = join_halves(*pieces)
        return carry

    lax.fori_loop(0, out_ref.shape[0], pack, 0, unroll=4)


def gather_rows(req, slab, n_ctx):
    return pl.pallas_call(
        gather_kernel,
        out_shape=jax.ShapeDtypeStruct((n_ctx, FEAT, LANES), jnp.bfloat16),
        in_specs=[
            pl.BlockSpec(memory_space=pltpu.SMEM),
            pl.BlockSpec(memory_space=pltpu.VMEM),
        ],
        out_specs=pl.BlockSpec(memory_space=pltpu.VMEM),
        compiler_params=pltpu.CompilerParams(vmem_limit_bytes=16 * 2**20),
        cost_estimate=pl.CostEstimate(flops=0, bytes_accessed=4 * 2**20, transcendentals=0),
        name="gather_rows",
    )(req, slab)


def compact_kernel(owner_ref, rank_ref, recv_ref, out_ref):
    for p in range(SEL // 2):
        a, b = 2 * p, 2 * p + 1
        out_ref[:, p * LANES : (p + 1) * LANES] = join_halves(
            recv_ref[owner_ref[a]], rank_ref[a], recv_ref[owner_ref[b]], rank_ref[b]
        )


def compact(owner, rank, recv):
    return pl.pallas_call(
        compact_kernel,
        out_shape=jax.ShapeDtypeStruct((FEAT, KEYS), jnp.bfloat16),
        in_specs=[
            pl.BlockSpec(memory_space=pltpu.SMEM),
            pl.BlockSpec(memory_space=pltpu.SMEM),
            pl.BlockSpec(memory_space=pltpu.VMEM),
        ],
        out_specs=pl.BlockSpec(memory_space=pltpu.VMEM),
        compiler_params=pltpu.CompilerParams(vmem_limit_bytes=16 * 2**20),
        cost_estimate=pl.CostEstimate(flops=0, bytes_accessed=2 * 2**20, transcendentals=0),
        name="compact",
    )(owner, rank, recv)


def attend_kernel(info_ref, pos_ref, q_ref, k0, k1, k2, k3, w_ref, out_ref, keys, sem):
    rows = q_ref.shape[0]

    @pl.when(pl.program_id(0) == 0)
    def _():
        copies = []
        for n, ref in enumerate((k0, k1, k2, k3)):
            part = lax.rem(info_ref[1] + XDIM - n, XDIM)
            place = pl.ds(pl.multiple_of(part * FEAT, 16), FEAT)
            copies.append(pltpu.make_async_copy(ref, keys.at[place, :], sem.at[n]))
        for copy in copies:
            copy.start()
        for copy in copies:
            copy.wait()

    tok = lax.broadcasted_iota(jnp.int32, (rows, 1), 0) % BLOCK
    query_pos = info_ref[0] + tok
    q = q_ref[...]
    width = 512
    scores = []
    for c in range(0, KEYS, width):
        s = jnp.dot(q, keys[:, c : c + width], preferred_element_type=jnp.float32)
        scores.append(jnp.where(pos_ref[:, c : c + width] <= query_pos, s, -jnp.inf))
    peak = jnp.max(functools.reduce(jnp.maximum, scores), axis=1, keepdims=True)
    total = jnp.zeros((rows, width), jnp.float32)
    acc = jnp.zeros((rows, LATENT), jnp.float32)
    for n, s in enumerate(scores):
        p = jnp.exp2((s - peak) * (SCALE * LOG2E))
        total = total + p
        acc = acc + lax.dot_general(
            p.astype(jnp.bfloat16),
            keys[:LATENT, n * width : (n + 1) * width],
            (((1,), (1,)), ((), ())),
            preferred_element_type=jnp.float32,
        )
    attended = (acc / jnp.sum(total, axis=1, keepdims=True)).astype(jnp.bfloat16)
    for n in range(rows // BLOCK):
        values = jnp.dot(attended[n * BLOCK : (n + 1) * BLOCK], w_ref[n], preferred_element_type=jnp.float32)
        out_ref[:, n * VHEAD : (n + 1) * VHEAD] = values.astype(jnp.bfloat16)


def attend(info, pos, q, chunks, w_uv):
    rows_all = q.shape[0]
    tile = 512
    heads = tile // BLOCK
    whole = pl.BlockSpec(memory_space=pl.ANY)
    return pl.pallas_call(
        attend_kernel,
        grid=(rows_all // tile,),
        out_shape=jax.ShapeDtypeStruct((BLOCK, rows_all // BLOCK * VHEAD), jnp.bfloat16),
        in_specs=[
            pl.BlockSpec(memory_space=pltpu.SMEM),
            pl.BlockSpec(pos.shape, lambda i: (0, 0)),
            pl.BlockSpec((tile, WIDTH), lambda i: (i, 0)),
            whole,
            whole,
            whole,
            whole,
            pl.BlockSpec((heads, LATENT, VHEAD), lambda i: (i, 0, 0)),
        ],
        out_specs=pl.BlockSpec((BLOCK, heads * VHEAD), lambda i: (0, i)),
        scratch_shapes=[pltpu.VMEM((WIDTH, KEYS), jnp.bfloat16), pltpu.SemaphoreType.DMA((XDIM,))],
        compiler_params=pltpu.CompilerParams(vmem_limit_bytes=32 * 2**20),
        cost_estimate=pl.CostEstimate(flops=5 * 10**9, bytes_accessed=8 * 2**20, transcendentals=2**21),
        name="attend",
    )(info, pos, q, *chunks, w_uv)


def project_kernel(info_ref, *refs):
    pieces, shards = refs[:YDIM], refs[YDIM : YDIM + ZDIM]
    out_ref, rows, w, row_sem, w_sem = refs[YDIM + ZDIM :]
    copies = []
    for n, ref in enumerate(pieces):
        slot = jnp.bitwise_and(info_ref[0] + YDIM - n, YDIM - 1) * LANES
        for side in range(2):
            start = slot + jnp.bitwise_xor(info_ref[2], side) * BLOCK
            place = pl.ds(pl.multiple_of(start, BLOCK), BLOCK)
            copies.append(
                pltpu.make_async_copy(
                    ref.at[pl.ds(side * BLOCK, BLOCK), :], rows.at[place, :], row_sem.at[2 * n + side]
                )
            )
    for n, ref in enumerate(shards):
        col = jnp.bitwise_and(info_ref[1] + n, ZDIM - 1) * VHEAD
        place = pl.ds(pl.multiple_of(col, VHEAD), VHEAD)
        copies.append(pltpu.make_async_copy(ref, w.at[:, place], w_sem.at[n]))
    for copy in copies:
        copy.start()
    for copy in copies:
        copy.wait()
    half = w.shape[1] // 2
    for side in range(2):
        out = jnp.dot(rows[...], w[:, side * half : (side + 1) * half], preferred_element_type=jnp.float32)
        out_ref[jnp.bitwise_xor(info_ref[2], side)] = out.astype(jnp.bfloat16)


def project(info, pieces, shards):
    depth, cols = shards[0].shape
    count = YDIM * pieces[0].shape[0]
    return pl.pallas_call(
        project_kernel,
        in_specs=[pl.BlockSpec(memory_space=pltpu.SMEM)] + [pl.BlockSpec(memory_space=pl.ANY)] * (YDIM + ZDIM),
        out_specs=pl.BlockSpec(memory_space=pltpu.VMEM),
        out_shape=jax.ShapeDtypeStruct((2, count, ZDIM * cols // 2), jnp.bfloat16),
        scratch_shapes=[
            pltpu.VMEM((count, depth), jnp.bfloat16),
            pltpu.VMEM((depth, ZDIM * cols), jnp.bfloat16),
            pltpu.SemaphoreType.DMA((2 * YDIM,)),
            pltpu.SemaphoreType.DMA((ZDIM,)),
        ],
        compiler_params=pltpu.CompilerParams(vmem_limit_bytes=20 * 2**20),
        cost_estimate=pl.CostEstimate(flops=10**9, bytes_accessed=6 * 2**20, transcendentals=0),
        name="project",
    )(info, *pieces, *shards)


def per_device(queries, latents, selected, w_uv, w_out):
    n_ctx = lax.axis_size("ctx")
    n_head = lax.axis_size("head")
    shard = lax.axis_index("ctx")
    head = lax.axis_index("head")
    core = jnp.bitwise_and(head, 1)
    x = lax.shift_right_logical(head, 1)
    y = lax.shift_right_logical(shard, 3)
    z = jnp.bitwise_and(shard, ZDIM - 1)
    tok_dev, heads_here, width = queries.shape
    blocks_dev = latents.shape[0] // BLOCK
    first_block = blocks_dev * n_ctx - (tok_dev // BLOCK) * n_ctx
    swap = [(i, i ^ 1) for i in range(n_head)]

    def along_x(value, d):
        return lax.ppermute(value, "head", [(i, (i + 2 * d) % n_head) for i in range(n_head)])

    def along_y(value, d):
        return lax.ppermute(value, "ctx", [(i, (i + ZDIM * d) % n_ctx) for i in range(n_ctx)])

    def along_z(value, d):
        return lax.ppermute(value, "ctx", [(i, i // ZDIM * ZDIM + (i + d) % ZDIM) for i in range(n_ctx)])

    picks = jnp.where(core == 0, selected[0], selected[1])
    owner = lax.shift_right_logical(picks, 6)
    local = jnp.bitwise_and(picks, blocks_dev - 1)
    order = jnp.arange(SEL, dtype=jnp.int32)
    same = (owner[:, None] == owner[None, :]) & (order[None, :] < order[:, None])
    rank = jnp.sum(same.astype(jnp.int32), axis=1)
    slot = owner * PER_OWNER + rank
    match = slot[:, None, None] == (
        jnp.arange(n_ctx, dtype=jnp.int32)[None, :, None] * PER_OWNER
        + jnp.arange(LANES, dtype=jnp.int32)[None, None, :] // BLOCK
    )
    wanted = jnp.sum(jnp.where(match, local[:, None, None], 0), axis=0).astype(jnp.bfloat16)
    req = lax.all_to_all(wanted, "ctx", split_axis=0, concat_axis=0, tiled=True)
    req = req[:, ::BLOCK].astype(jnp.int32).reshape(-1)

    slab = lax.dynamic_slice_in_dim(latents.T, x * FEAT, FEAT, axis=0)
    up1, down1 = along_z(w_out, 1), along_z(w_out, -1)
    req, up1, down1 = lax.optimization_barrier((req, up1, down1))
    piece = gather_rows(req, slab, n_ctx)
    up2, down2 = along_z(up1, 1), along_z(down1, -1)
    recv = lax.all_to_all(piece, "ctx", split_axis=0, concat_axis=0, tiled=True)

    by_head = queries.transpose(1, 0, 2)
    mine = lax.dynamic_slice_in_dim(by_head, core * BLOCK, BLOCK, axis=1)
    theirs = lax.dynamic_slice_in_dim(by_head, (1 - core) * BLOCK, BLOCK, axis=1)
    got = lax.ppermute(theirs, "head", swap)
    uv_other = lax.ppermute(w_uv, "head", swap)
    q = jnp.concatenate([mine, got], axis=0).reshape(2 * heads_here * BLOCK, width)
    uv_pair = jnp.concatenate([w_uv, uv_other], axis=0)

    chunk = compact(owner, rank, recv)
    chunk, up2, down2 = lax.optimization_barrier((chunk, up2, down2))
    chunks = [chunk] + [along_x(chunk, d) for d in range(1, XDIM)]
    up3, down3 = along_z(up2, 1), along_z(down2, -1)
    chunks[3], up3, down3 = lax.optimization_barrier((chunks[3], up3, down3))
    up4 = along_z(up3, 1)
    pos = (picks[:, None] * BLOCK + jnp.arange(BLOCK, dtype=jnp.int32)[None, :]).reshape(1, -1)
    first = (first_block + shard * (tok_dev // BLOCK) + core) * BLOCK
    values = attend(jnp.stack([first, x]), pos, q, chunks, uv_pair)

    half = heads_here * VHEAD
    values = jnp.concatenate([values[:, :half], lax.ppermute(values[:, half:], "head", swap)], axis=0)
    pieces = [values] + [along_y(values, d) for d in range(1, YDIM)]
    info = jnp.stack([jnp.bitwise_and(y - x, YDIM - 1), z, core])
    partial_rows = project(info, pieces, [w_out, down1, down2, down3, up4, up3, up2, up1])
    other = lax.ppermute(partial_rows[1], "head", swap)
    both = (partial_rows[0].astype(jnp.float32) + other.astype(jnp.float32)).astype(jnp.bfloat16)
    both = both.reshape(YDIM, tok_dev, -1)
    total = both[0].astype(jnp.float32)
    for d in range(1, XDIM):
        total = total + along_x(both[d], d).astype(jnp.float32)
    total = total.astype(jnp.bfloat16)
    route = []
    for c in range(n_ctx):
        for h in range(n_head):
            route.append((c * n_head + h, (h // 2 * ZDIM + c % ZDIM) * n_head + c // ZDIM * 2 + h % 2))
    return lax.ppermute(total, ("ctx", "head"), route)


def solution(mesh):
    return jax.shard_map(
        per_device,
        mesh=mesh,
        in_specs=(
            P("ctx", "head", None),
            P("ctx", None),
            P("ctx", None),
            P("head", None, None),
            P("head", "ctx"),
        ),
        out_specs=P("ctx", "head"),
        check_vma=False,
    )
```

```python
import functools

import jax
import jax.numpy as jnp
from jax import lax
from jax.experimental import pallas as pl
from jax.experimental.pallas import tpu as pltpu
from jax.sharding import PartitionSpec as P

LATENT = 512
ROPE = 64
WIDTH = LATENT + ROPE
VHEAD = 128
BLOCK = 64
SEL = 32
KEYS = SEL * BLOCK
PER_OWNER = 2
XDIM = 4
YDIM = 4
GROUP = 2
ZDIM = 8
FEAT = WIDTH // XDIM
LANES = 2 * BLOCK
SCALE = 192.0 ** (-0.5)
LOG2E = 1.4426950408889634


def join_halves(a, a_half, b, b_half):
    low = jnp.where(a_half == 0, a[:, :BLOCK], a[:, BLOCK:])
    high = jnp.where(b_half == 0, b[:, :BLOCK], b[:, BLOCK:])
    return jnp.concatenate([low, high], axis=1)


def gather_kernel(req_ref, slab_ref, out_ref):
    def pack(i, carry):
        pieces = []
        for side in range(2):
            block = req_ref[2 * i + side]
            col = pl.multiple_of(lax.shift_right_logical(block, 1) * LANES, LANES)
            pieces += [slab_ref[:, pl.ds(col, LANES)], jnp.bitwise_and(block, 1)]
        out_ref[i] = join_halves(*pieces)
        return carry

    lax.fori_loop(0, out_ref.shape[0], pack, 0, unroll=4)


def gather_rows(req, slab, n_ctx):
    return pl.pallas_call(
        gather_kernel,
        out_shape=jax.ShapeDtypeStruct((n_ctx, FEAT, LANES), jnp.bfloat16),
        in_specs=[
            pl.BlockSpec(memory_space=pltpu.SMEM),
            pl.BlockSpec(memory_space=pltpu.VMEM),
        ],
        out_specs=pl.BlockSpec(memory_space=pltpu.VMEM),
        compiler_params=pltpu.CompilerParams(vmem_limit_bytes=16 * 2**20),
        cost_estimate=pl.CostEstimate(flops=0, bytes_accessed=4 * 2**20, transcendentals=0),
        name="gather_rows",
    )(req, slab)


def compact_kernel(owner_ref, rank_ref, recv_ref, out_ref):
    for p in range(SEL // 2):
        a, b = 2 * p, 2 * p + 1
        out_ref[:, p * LANES : (p + 1) * LANES] = join_halves(
            recv_ref[owner_ref[a]], rank_ref[a], recv_ref[owner_ref[b]], rank_ref[b]
        )


def compact(owner, rank, recv):
    return pl.pallas_call(
        compact_kernel,
        out_shape=jax.ShapeDtypeStruct((FEAT, KEYS), jnp.bfloat16),
        in_specs=[
            pl.BlockSpec(memory_space=pltpu.SMEM),
            pl.BlockSpec(memory_space=pltpu.SMEM),
            pl.BlockSpec(memory_space=pltpu.VMEM),
        ],
        out_specs=pl.BlockSpec(memory_space=pltpu.VMEM),
        compiler_params=pltpu.CompilerParams(vmem_limit_bytes=16 * 2**20),
        cost_estimate=pl.CostEstimate(flops=0, bytes_accessed=2 * 2**20, transcendentals=0),
        name="compact",
    )(owner, rank, recv)


def attend_kernel(info_ref, pos_ref, q_ref, k0, k1, k2, k3, w_ref, out_ref, keys, sem):
    rows = q_ref.shape[0]

    @pl.when(pl.program_id(0) == 0)
    def _():
        copies = []
        for n, ref in enumerate((k0, k1, k2, k3)):
            part = lax.rem(info_ref[1] + XDIM - n, XDIM)
            place = pl.ds(pl.multiple_of(part * FEAT, 16), FEAT)
            copies.append(pltpu.make_async_copy(ref, keys.at[place, :], sem.at[n]))
        for copy in copies:
            copy.start()
        for copy in copies:
            copy.wait()

    tok = lax.broadcasted_iota(jnp.int32, (rows, 1), 0) % BLOCK
    query_pos = info_ref[0] + tok
    q = q_ref[...]
    width = 512
    scores = []
    for c in range(0, KEYS, width):
        s = jnp.dot(q, keys[:, c : c + width], preferred_element_type=jnp.float32)
        scores.append(jnp.where(pos_ref[:, c : c + width] <= query_pos, s, -jnp.inf))
    peak = jnp.max(functools.reduce(jnp.maximum, scores), axis=1, keepdims=True)
    total = jnp.zeros((rows, width), jnp.float32)
    acc = jnp.zeros((rows, LATENT), jnp.float32)
    for n, s in enumerate(scores):
        p = jnp.exp2((s - peak) * (SCALE * LOG2E))
        total = total + p
        acc = acc + lax.dot_general(
            p.astype(jnp.bfloat16),
            keys[:LATENT, n * width : (n + 1) * width],
            (((1,), (1,)), ((), ())),
            preferred_element_type=jnp.float32,
        )
    attended = (acc / jnp.sum(total, axis=1, keepdims=True)).astype(jnp.bfloat16)
    for n in range(rows // BLOCK):
        values = jnp.dot(attended[n * BLOCK : (n + 1) * BLOCK], w_ref[n], preferred_element_type=jnp.float32)
        out_ref[:, n * VHEAD : (n + 1) * VHEAD] = values.astype(jnp.bfloat16)


def attend(info, pos, q, chunks, w_uv):
    rows_all = q.shape[0]
    tile = 512
    heads = tile // BLOCK
    whole = pl.BlockSpec(memory_space=pl.ANY)
    return pl.pallas_call(
        attend_kernel,
        grid=(rows_all // tile,),
        out_shape=jax.ShapeDtypeStruct((BLOCK, rows_all // BLOCK * VHEAD), jnp.bfloat16),
        in_specs=[
            pl.BlockSpec(memory_space=pltpu.SMEM),
            pl.BlockSpec(pos.shape, lambda i: (0, 0)),
            pl.BlockSpec((tile, WIDTH), lambda i: (i, 0)),
            whole,
            whole,
            whole,
            whole,
            pl.BlockSpec((heads, LATENT, VHEAD), lambda i: (i, 0, 0)),
        ],
        out_specs=pl.BlockSpec((BLOCK, heads * VHEAD), lambda i: (0, i)),
        scratch_shapes=[pltpu.VMEM((WIDTH, KEYS), jnp.bfloat16), pltpu.SemaphoreType.DMA((XDIM,))],
        compiler_params=pltpu.CompilerParams(vmem_limit_bytes=32 * 2**20),
        cost_estimate=pl.CostEstimate(flops=5 * 10**9, bytes_accessed=8 * 2**20, transcendentals=2**21),
        name="attend",
    )(info, pos, q, *chunks, w_uv)


def project_kernel(info_ref, *refs):
    pieces, shards = refs[:GROUP], refs[GROUP : GROUP + ZDIM]
    out_ref, rows, w, row_sem, w_sem = refs[GROUP + ZDIM :]
    x, y, z, core = (info_ref[n] for n in range(4))
    copies = []
    for n, ref in enumerate(pieces):
        for side in range(2):
            start = n * LANES + jnp.bitwise_xor(core, side) * BLOCK
            place = pl.ds(pl.multiple_of(start, BLOCK), BLOCK)
            copies.append(
                pltpu.make_async_copy(
                    ref.at[pl.ds(side * BLOCK, BLOCK), :], rows.at[place, :], row_sem.at[2 * n + side]
                )
            )
    for n, ref in enumerate(shards):
        for j in range(2):
            col = j * ZDIM * VHEAD + jnp.bitwise_and(z + n, ZDIM - 1) * VHEAD
            place = pl.ds(pl.multiple_of(col, VHEAD), VHEAD)
            copies.append(
                pltpu.make_async_copy(
                    ref.at[:, pl.ds(j * VHEAD, VHEAD)], w.at[:, place], w_sem.at[2 * n + j]
                )
            )
    for copy in copies:
        copy.start()
    for copy in copies:
        copy.wait()
    half = out_ref.shape[3]
    upper = lax.shift_right_logical(y, 1)
    for j in range(2):
        for side in range(2):
            col = (2 * j + side) * half
            out = jnp.dot(rows[...], w[:, col : col + half], preferred_element_type=jnp.float32)
            out = out.astype(jnp.bfloat16)
            for n in range(GROUP):
                to = jnp.bitwise_xor(2 * upper + j, 2 * n)
                slot = jnp.bitwise_and(to + XDIM - x, XDIM - 1)
                out_ref[jnp.bitwise_xor(core, side), slot] = out[n * LANES : (n + 1) * LANES]


def project(info, pieces, shards):
    depth, cols = shards[0].shape
    count = GROUP * LANES
    return pl.pallas_call(
        project_kernel,
        in_specs=[pl.BlockSpec(memory_space=pltpu.SMEM)] + [pl.BlockSpec(memory_space=pl.ANY)] * (GROUP + ZDIM),
        out_specs=pl.BlockSpec(memory_space=pltpu.VMEM),
        out_shape=jax.ShapeDtypeStruct((2, XDIM, LANES, ZDIM * cols // 4), jnp.bfloat16),
        scratch_shapes=[
            pltpu.VMEM((count, depth), jnp.bfloat16),
            pltpu.VMEM((depth, ZDIM * cols), jnp.bfloat16),
            pltpu.SemaphoreType.DMA((2 * GROUP,)),
            pltpu.SemaphoreType.DMA((2 * ZDIM,)),
        ],
        compiler_params=pltpu.CompilerParams(vmem_limit_bytes=20 * 2**20),
        cost_estimate=pl.CostEstimate(flops=10**9, bytes_accessed=6 * 2**20, transcendentals=0),
        name="project",
    )(info, *pieces, *shards)


def per_device(queries, latents, selected, w_uv, w_out):
    n_ctx = lax.axis_size("ctx")
    n_head = lax.axis_size("head")
    shard = lax.axis_index("ctx")
    head = lax.axis_index("head")
    core = jnp.bitwise_and(head, 1)
    x = lax.shift_right_logical(head, 1)
    y = lax.shift_right_logical(shard, 3)
    z = jnp.bitwise_and(shard, ZDIM - 1)
    tok_dev, heads_here, width = queries.shape
    blocks_dev = latents.shape[0] // BLOCK
    first_block = blocks_dev * n_ctx - (tok_dev // BLOCK) * n_ctx
    swap = [(i, i ^ 1) for i in range(n_head)]

    def along_x(value, d):
        return lax.ppermute(value, "head", [(i, (i + 2 * d) % n_head) for i in range(n_head)])

    def along_y(value, d):
        return lax.ppermute(value, "ctx", [(i, (i + ZDIM * d) % n_ctx) for i in range(n_ctx)])

    def along_z(value, d):
        return lax.ppermute(value, "ctx", [(i, i // ZDIM * ZDIM + (i + d) % ZDIM) for i in range(n_ctx)])

    picks = jnp.where(core == 0, selected[0], selected[1])
    owner = lax.shift_right_logical(picks, 6)
    local = jnp.bitwise_and(picks, blocks_dev - 1)
    order = jnp.arange(SEL, dtype=jnp.int32)
    same = (owner[:, None] == owner[None, :]) & (order[None, :] < order[:, None])
    rank = jnp.sum(same.astype(jnp.int32), axis=1)
    slot = owner * PER_OWNER + rank
    match = slot[:, None, None] == (
        jnp.arange(n_ctx, dtype=jnp.int32)[None, :, None] * PER_OWNER
        + jnp.arange(LANES, dtype=jnp.int32)[None, None, :] // BLOCK
    )
    wanted = jnp.sum(jnp.where(match, local[:, None, None], 0), axis=0).astype(jnp.bfloat16)
    req = lax.all_to_all(wanted, "ctx", split_axis=0, concat_axis=0, tiled=True)
    req = req[:, ::BLOCK].astype(jnp.int32).reshape(-1)

    slab = lax.dynamic_slice_in_dim(latents.T, x * FEAT, FEAT, axis=0)
    up1, down1 = along_z(w_out, 1), along_z(w_out, -1)
    req, near, up1, down1 = lax.optimization_barrier((req, w_out, up1, down1))

    def pair(own):
        peer = lax.ppermute(own, "ctx", [(i, i ^ ZDIM) for i in range(n_ctx)])
        even = jnp.bitwise_and(y, 1) == 0
        return jnp.where(even, jnp.concatenate([own, peer], axis=1), jnp.concatenate([peer, own], axis=1))

    piece = gather_rows(req, slab, n_ctx)
    recv = lax.all_to_all(piece, "ctx", split_axis=0, concat_axis=0, tiled=True)

    by_head = queries.transpose(1, 0, 2)
    mine = lax.dynamic_slice_in_dim(by_head, core * BLOCK, BLOCK, axis=1)
    theirs = lax.dynamic_slice_in_dim(by_head, (1 - core) * BLOCK, BLOCK, axis=1)
    got = lax.ppermute(theirs, "head", swap)
    uv_other = lax.ppermute(w_uv, "head", swap)
    q = jnp.concatenate([mine, got], axis=0).reshape(2 * heads_here * BLOCK, width)
    uv_pair = jnp.concatenate([w_uv, uv_other], axis=0)

    chunk = compact(owner, rank, recv)
    w_pair, up1, down1 = pair(near), pair(up1), pair(down1)
    chunk, w_pair, up1, down1 = lax.optimization_barrier((chunk, w_pair, up1, down1))
    chunks = [chunk] + [along_x(chunk, d) for d in range(1, XDIM)]
    up2, down2 = along_z(up1, 1), along_z(down1, -1)
    up3, down3 = along_z(up2, 1), along_z(down2, -1)
    chunks[3], up3, down3 = lax.optimization_barrier((chunks[3], up3, down3))
    up4 = along_z(up3, 1)
    pos = (picks[:, None] * BLOCK + jnp.arange(BLOCK, dtype=jnp.int32)[None, :]).reshape(1, -1)
    first = (first_block + shard * (tok_dev // BLOCK) + core) * BLOCK
    values = attend(jnp.stack([first, x]), pos, q, chunks, uv_pair)

    half = heads_here * VHEAD
    values = jnp.concatenate([values[:, :half], lax.ppermute(values[:, half:], "head", swap)], axis=0)
    pieces = [values, along_y(values, 2)]
    info = jnp.stack([x, y, z, core])
    partial_rows = project(info, pieces, [w_pair, down1, down2, down3, up4, up3, up2, up1])
    other = lax.ppermute(partial_rows[1], "head", swap)
    both = (partial_rows[0].astype(jnp.float32) + other.astype(jnp.float32)).astype(jnp.bfloat16)
    total = both[0].astype(jnp.float32)
    for d in range(1, XDIM):
        total = total + along_x(both[d], d).astype(jnp.float32)
    total = total.astype(jnp.bfloat16)
    route = []
    for c in range(n_ctx):
        for h in range(n_head):
            if c // (2 * ZDIM) != h // 4:
                route.append((c * n_head + h, (c ^ (2 * ZDIM)) * n_head + (h ^ 4)))
    moved = lax.ppermute(total, ("ctx", "head"), route)
    return jnp.where(lax.shift_right_logical(y, 1) == lax.shift_right_logical(x, 1), total, moved)


def solution(mesh):
    return jax.shard_map(
        per_device,
        mesh=mesh,
        in_specs=(
            P("ctx", "head", None),
            P("ctx", None),
            P("ctx", None),
            P("head", None, None),
            P("head", "ctx"),
        ),
        out_specs=P("ctx", "head"),
        check_vma=False,
    )
```

```python
import functools

import jax
import jax.numpy as jnp
from jax import lax
from jax.experimental import pallas as pl
from jax.experimental.pallas import tpu as pltpu
from jax.sharding import PartitionSpec as P

LATENT = 512
ROPE = 64
WIDTH = LATENT + ROPE
VHEAD = 128
BLOCK = 64
SEL = 32
KEYS = SEL * BLOCK
PER_OWNER = 2
XDIM = 4
YDIM = 4
GROUP = 2
ZDIM = 8
FEAT = WIDTH // XDIM
LANES = 2 * BLOCK
SCALE = 192.0 ** (-0.5)
LOG2E = 1.4426950408889634


def join_halves(a, a_half, b, b_half):
    low = jnp.where(a_half == 0, a[:, :BLOCK], a[:, BLOCK:])
    high = jnp.where(b_half == 0, b[:, :BLOCK], b[:, BLOCK:])
    return jnp.concatenate([low, high], axis=1)


def gather_kernel(req_ref, slab_ref, out_ref):
    def pack(i, carry):
        pieces = []
        for side in range(2):
            block = req_ref[2 * i + side]
            col = pl.multiple_of(lax.shift_right_logical(block, 1) * LANES, LANES)
            pieces += [slab_ref[:, pl.ds(col, LANES)], jnp.bitwise_and(block, 1)]
        out_ref[i] = join_halves(*pieces)
        return carry

    lax.fori_loop(0, out_ref.shape[0], pack, 0, unroll=4)


def gather_rows(req, slab, n_ctx):
    return pl.pallas_call(
        gather_kernel,
        out_shape=jax.ShapeDtypeStruct((n_ctx, FEAT, LANES), jnp.bfloat16),
        in_specs=[
            pl.BlockSpec(memory_space=pltpu.SMEM),
            pl.BlockSpec(memory_space=pltpu.VMEM),
        ],
        out_specs=pl.BlockSpec(memory_space=pltpu.VMEM),
        compiler_params=pltpu.CompilerParams(vmem_limit_bytes=16 * 2**20),
        cost_estimate=pl.CostEstimate(flops=0, bytes_accessed=4 * 2**20, transcendentals=0),
        name="gather_rows",
    )(req, slab)


def compact_kernel(owner_ref, rank_ref, recv_ref, out_ref):
    for p in range(SEL // 2):
        a, b = 2 * p, 2 * p + 1
        out_ref[:, p * LANES : (p + 1) * LANES] = join_halves(
            recv_ref[owner_ref[a]], rank_ref[a], recv_ref[owner_ref[b]], rank_ref[b]
        )


def compact(owner, rank, recv):
    return pl.pallas_call(
        compact_kernel,
        out_shape=jax.ShapeDtypeStruct((FEAT, KEYS), jnp.bfloat16),
        in_specs=[
            pl.BlockSpec(memory_space=pltpu.SMEM),
            pl.BlockSpec(memory_space=pltpu.SMEM),
            pl.BlockSpec(memory_space=pltpu.VMEM),
        ],
        out_specs=pl.BlockSpec(memory_space=pltpu.VMEM),
        compiler_params=pltpu.CompilerParams(vmem_limit_bytes=16 * 2**20),
        cost_estimate=pl.CostEstimate(flops=0, bytes_accessed=2 * 2**20, transcendentals=0),
        name="compact",
    )(owner, rank, recv)


def attend_kernel(info_ref, pos_ref, q_ref, k0, k1, k2, k3, w_ref, out_ref, keys, sem):
    rows = q_ref.shape[0]

    @pl.when(pl.program_id(0) == 0)
    def _():
        copies = []
        for n, ref in enumerate((k0, k1, k2, k3)):
            part = lax.rem(info_ref[1] + XDIM - n, XDIM)
            place = pl.ds(pl.multiple_of(part * FEAT, 16), FEAT)
            copies.append(pltpu.make_async_copy(ref, keys.at[place, :], sem.at[n]))
        for copy in copies:
            copy.start()
        for copy in copies:
            copy.wait()

    tok = lax.broadcasted_iota(jnp.int32, (rows, 1), 0) % BLOCK
    query_pos = info_ref[0] + tok
    q = q_ref[...]
    width = 512
    scores = []
    for c in range(0, KEYS, width):
        s = jnp.dot(q, keys[:, c : c + width], preferred_element_type=jnp.float32)
        scores.append(jnp.where(pos_ref[:, c : c + width] <= query_pos, s, -jnp.inf))
    peak = jnp.max(functools.reduce(jnp.maximum, scores), axis=1, keepdims=True)
    total = jnp.zeros((rows, width), jnp.float32)
    acc = jnp.zeros((rows, LATENT), jnp.float32)
    for n, s in enumerate(scores):
        p = jnp.exp2((s - peak) * (SCALE * LOG2E))
        total = total + p
        acc = acc + lax.dot_general(
            p.astype(jnp.bfloat16),
            keys[:LATENT, n * width : (n + 1) * width],
            (((1,), (1,)), ((), ())),
            preferred_element_type=jnp.float32,
        )
    attended = (acc / jnp.sum(total, axis=1, keepdims=True)).astype(jnp.bfloat16)
    for n in range(rows // BLOCK):
        values = jnp.dot(attended[n * BLOCK : (n + 1) * BLOCK], w_ref[n], preferred_element_type=jnp.float32)
        out_ref[:, n * VHEAD : (n + 1) * VHEAD] = values.astype(jnp.bfloat16)


def attend(info, pos, q, chunks, w_uv):
    rows_all = q.shape[0]
    tile = 512
    heads = tile // BLOCK
    whole = pl.BlockSpec(memory_space=pl.ANY)
    return pl.pallas_call(
        attend_kernel,
        grid=(rows_all // tile,),
        out_shape=jax.ShapeDtypeStruct((BLOCK, rows_all // BLOCK * VHEAD), jnp.bfloat16),
        in_specs=[
            pl.BlockSpec(memory_space=pltpu.SMEM),
            pl.BlockSpec(pos.shape, lambda i: (0, 0)),
            pl.BlockSpec((tile, WIDTH), lambda i: (i, 0)),
            whole,
            whole,
            whole,
            whole,
            pl.BlockSpec((heads, LATENT, VHEAD), lambda i: (i, 0, 0)),
        ],
        out_specs=pl.BlockSpec((BLOCK, heads * VHEAD), lambda i: (0, i)),
        scratch_shapes=[pltpu.VMEM((WIDTH, KEYS), jnp.bfloat16), pltpu.SemaphoreType.DMA((XDIM,))],
        compiler_params=pltpu.CompilerParams(vmem_limit_bytes=32 * 2**20),
        cost_estimate=pl.CostEstimate(flops=5 * 10**9, bytes_accessed=8 * 2**20, transcendentals=2**21),
        name="attend",
    )(info, pos, q, *chunks, w_uv)


def project_kernel(side, info_ref, *refs):
    pieces, shards = refs[:GROUP], refs[GROUP : GROUP + ZDIM]
    out_ref, rows, w, row_sem, w_sem = refs[GROUP + ZDIM :]
    x, y, z, core = (info_ref[n] for n in range(4))
    wanted = jnp.bitwise_xor(core, side)
    per_half = ZDIM // 2
    row_copies = []
    for n, ref in enumerate(pieces):
        for half in range(2):
            start = n * LANES + jnp.bitwise_xor(core, half) * BLOCK
            place = pl.ds(pl.multiple_of(start, BLOCK), BLOCK)
            row_copies.append(
                pltpu.make_async_copy(
                    ref.at[pl.ds(half * BLOCK, BLOCK), :], rows.at[place, :], row_sem.at[2 * n + half]
                )
            )

    def shard_copies(n):
        position = jnp.bitwise_and(jnp.bitwise_and(z + n, ZDIM - 1), per_half - 1) * VHEAD
        found = []
        for j in range(2):
            place = pl.ds(pl.multiple_of(j * per_half * VHEAD + position, VHEAD), VHEAD)
            found.append(
                pltpu.make_async_copy(
                    shards[n].at[:, pl.ds(j * VHEAD, VHEAD)], w.at[:, place], w_sem.at[2 * n + j]
                )
            )
        return found

    for copy in row_copies:
        copy.start()
    here = [jnp.bitwise_and(z + n, ZDIM - 1) // per_half == wanted for n in range(ZDIM)]
    for n in range(ZDIM):

        @pl.when(here[n])
        def _():
            for copy in shard_copies(n):
                copy.start()

    for copy in row_copies:
        copy.wait()
    for n in range(ZDIM):

        @pl.when(here[n])
        def _():
            for copy in shard_copies(n):
                copy.wait()

    cols = out_ref.shape[2]
    upper = lax.shift_right_logical(y, 1)
    for j in range(2):
        out = jnp.dot(rows[...], w[:, j * cols : (j + 1) * cols], preferred_element_type=jnp.float32)
        out = out.astype(jnp.bfloat16)
        for n in range(GROUP):
            to = jnp.bitwise_xor(2 * upper + j, 2 * n)
            out_ref[jnp.bitwise_and(to + XDIM - x, XDIM - 1)] = out[n * LANES : (n + 1) * LANES]


def project(side, info, pieces, shards):
    depth, cols = shards[0].shape
    count = GROUP * LANES
    return pl.pallas_call(
        functools.partial(project_kernel, side),
        in_specs=[pl.BlockSpec(memory_space=pltpu.SMEM)] + [pl.BlockSpec(memory_space=pl.ANY)] * (GROUP + ZDIM),
        out_specs=pl.BlockSpec(memory_space=pltpu.VMEM),
        out_shape=jax.ShapeDtypeStruct((XDIM, LANES, ZDIM * cols // 4), jnp.bfloat16),
        scratch_shapes=[
            pltpu.VMEM((count, depth), jnp.bfloat16),
            pltpu.VMEM((depth, ZDIM * cols // 2), jnp.bfloat16),
            pltpu.SemaphoreType.DMA((2 * GROUP,)),
            pltpu.SemaphoreType.DMA((2 * ZDIM,)),
        ],
        compiler_params=pltpu.CompilerParams(vmem_limit_bytes=16 * 2**20),
        cost_estimate=pl.CostEstimate(flops=2 * 10**9, bytes_accessed=8 * 2**20, transcendentals=0),
        name=("project_own", "project_other")[side],
    )(info, *pieces, *shards)


def after(value, other):
    return lax.optimization_barrier((value, other))[0]


def per_device(queries, latents, selected, w_uv, w_out):
    n_ctx = lax.axis_size("ctx")
    n_head = lax.axis_size("head")
    shard = lax.axis_index("ctx")
    head = lax.axis_index("head")
    core = jnp.bitwise_and(head, 1)
    x = lax.shift_right_logical(head, 1)
    y = lax.shift_right_logical(shard, 3)
    z = jnp.bitwise_and(shard, ZDIM - 1)
    tok_dev, heads_here, width = queries.shape
    blocks_dev = latents.shape[0] // BLOCK
    first_block = blocks_dev * n_ctx - (tok_dev // BLOCK) * n_ctx
    swap = [(i, i ^ 1) for i in range(n_head)]

    def along_x(value, d):
        return lax.ppermute(value, "head", [(i, (i + 2 * d) % n_head) for i in range(n_head)])

    def along_y(value, d):
        return lax.ppermute(value, "ctx", [(i, (i + ZDIM * d) % n_ctx) for i in range(n_ctx)])

    def along_z(value, d):
        return lax.ppermute(value, "ctx", [(i, i // ZDIM * ZDIM + (i + d) % ZDIM) for i in range(n_ctx)])

    picks = jnp.where(core == 0, selected[0], selected[1])
    owner = lax.shift_right_logical(picks, 6)
    local = jnp.bitwise_and(picks, blocks_dev - 1)
    order = jnp.arange(SEL, dtype=jnp.int32)
    same = (owner[:, None] == owner[None, :]) & (order[None, :] < order[:, None])
    rank = jnp.sum(same.astype(jnp.int32), axis=1)
    slot = owner * PER_OWNER + rank
    match = slot[:, None, None] == (
        jnp.arange(n_ctx, dtype=jnp.int32)[None, :, None] * PER_OWNER
        + jnp.arange(LANES, dtype=jnp.int32)[None, None, :] // BLOCK
    )
    wanted = jnp.sum(jnp.where(match, local[:, None, None], 0), axis=0).astype(jnp.bfloat16)
    req = lax.all_to_all(wanted, "ctx", split_axis=0, concat_axis=0, tiled=True)
    req = req[:, ::BLOCK].astype(jnp.int32).reshape(-1)

    slab = lax.dynamic_slice_in_dim(latents.T, x * FEAT, FEAT, axis=0)
    up1, down1 = along_z(w_out, 1), along_z(w_out, -1)
    req, near, up1, down1 = lax.optimization_barrier((req, w_out, up1, down1))

    def peer_of(own):
        return lax.ppermute(own, "ctx", [(i, i ^ ZDIM) for i in range(n_ctx)])

    def pair(own, peer):
        even = jnp.bitwise_and(y, 1) == 0
        return jnp.where(even, jnp.concatenate([own, peer], axis=1), jnp.concatenate([peer, own], axis=1))

    piece = gather_rows(req, slab, n_ctx)
    recv = lax.all_to_all(piece, "ctx", split_axis=0, concat_axis=0, tiled=True)

    by_head = queries.transpose(1, 0, 2)
    mine = lax.dynamic_slice_in_dim(by_head, core * BLOCK, BLOCK, axis=1)
    theirs = lax.dynamic_slice_in_dim(by_head, (1 - core) * BLOCK, BLOCK, axis=1)
    got = lax.ppermute(theirs, "head", swap)
    uv_other = lax.ppermute(w_uv, "head", swap)
    q = jnp.concatenate([mine, got], axis=0).reshape(2 * heads_here * BLOCK, width)
    uv_pair = jnp.concatenate([w_uv, uv_other], axis=0)

    chunk = compact(owner, rank, recv)
    up1, down1 = pair(up1, peer_of(up1)), pair(down1, peer_of(down1))
    chunk, up1, down1 = lax.optimization_barrier((chunk, up1, down1))
    chunks = [chunk] + [along_x(chunk, d) for d in range(1, XDIM)]
    up2, down2 = along_z(up1, 1), along_z(down1, -1)
    up3, down3 = along_z(up2, 1), along_z(down2, -1)
    w_peer = peer_of(after(near, up2))
    chunks[3], w_peer, up3, down3 = lax.optimization_barrier((chunks[3], w_peer, up3, down3))
    w_pair = pair(near, w_peer)
    up4 = along_z(up3, 1)
    pos = (picks[:, None] * BLOCK + jnp.arange(BLOCK, dtype=jnp.int32)[None, :]).reshape(1, -1)
    first = (first_block + shard * (tok_dev // BLOCK) + core) * BLOCK
    values = attend(jnp.stack([first, x]), pos, q, chunks, uv_pair)

    half = heads_here * VHEAD
    values = jnp.concatenate([values[:, :half], lax.ppermute(values[:, half:], "head", swap)], axis=0)
    pieces = [values, along_y(values, 2)]
    info = jnp.stack([x, y, z, core])
    shards = [w_pair, down1, down2, down3, up4, up3, up2, up1]
    sent = project(1, info, pieces, shards)
    other = lax.ppermute(sent, "head", swap)
    kept = project(0, info, pieces, shards)
    both = (kept.astype(jnp.float32) + other.astype(jnp.float32)).astype(jnp.bfloat16)
    total = both[0].astype(jnp.float32)
    for d in range(1, XDIM):
        total = total + along_x(both[d], d).astype(jnp.float32)
    total = total.astype(jnp.bfloat16)
    route = []
    for c in range(n_ctx):
        for h in range(n_head):
            if c // (2 * ZDIM) != h // 4:
                route.append((c * n_head + h, (c ^ (2 * ZDIM)) * n_head + (h ^ 4)))
    moved = lax.ppermute(total, ("ctx", "head"), route)
    return jnp.where(lax.shift_right_logical(y, 1) == lax.shift_right_logical(x, 1), total, moved)


def solution(mesh):
    return jax.shard_map(
        per_device,
        mesh=mesh,
        in_specs=(
            P("ctx", "head", None),
            P("ctx", None),
            P("ctx", None),
            P("head", None, None),
            P("head", "ctx"),
        ),
        out_specs=P("ctx", "head"),
        check_vma=False,
    )
```

```python
import functools

import jax
import jax.numpy as jnp
from jax import lax
from jax.experimental import pallas as pl
from jax.experimental.pallas import tpu as pltpu
from jax.sharding import PartitionSpec as P

LATENT = 512
ROPE = 64
WIDTH = LATENT + ROPE
VHEAD = 128
BLOCK = 64
SEL = 32
KEYS = SEL * BLOCK
PER_OWNER = 2
XDIM = 4
YDIM = 4
GROUP = 2
ZDIM = 8
FEAT = WIDTH // XDIM
LANES = 2 * BLOCK
SCALE = 192.0 ** (-0.5)
LOG2E = 1.4426950408889634


def join_halves(a, a_half, b, b_half):
    lane = lax.broadcasted_iota(jnp.int32, a.shape, 1)
    low = pltpu.roll(a.astype(jnp.float32), a_half * BLOCK, 1)
    high = pltpu.roll(b.astype(jnp.float32), (1 - b_half) * BLOCK, 1)
    return jnp.where(lane < BLOCK, low, high).astype(a.dtype)


def gather_kernel(req_ref, slab_ref, out_ref):
    def pack(i, carry):
        pieces = []
        for side in range(2):
            block = req_ref[2 * i + side]
            col = pl.multiple_of(lax.shift_right_logical(block, 1) * LANES, LANES)
            pieces += [slab_ref[:, pl.ds(col, LANES)], jnp.bitwise_and(block, 1)]
        out_ref[i] = join_halves(*pieces)
        return carry

    lax.fori_loop(0, out_ref.shape[0], pack, 0, unroll=8)


def gather_rows(req, slab, n_ctx):
    return pl.pallas_call(
        gather_kernel,
        out_shape=jax.ShapeDtypeStruct((n_ctx, FEAT, LANES), jnp.bfloat16),
        in_specs=[
            pl.BlockSpec(memory_space=pltpu.SMEM),
            pl.BlockSpec(memory_space=pltpu.VMEM),
        ],
        out_specs=pl.BlockSpec(memory_space=pltpu.VMEM),
        compiler_params=pltpu.CompilerParams(vmem_limit_bytes=16 * 2**20),
        cost_estimate=pl.CostEstimate(flops=0, bytes_accessed=4 * 2**20, transcendentals=0),
        name="gather_rows",
    )(req, slab)


def compact_kernel(owner_ref, rank_ref, recv_ref, out_ref):
    for p in range(SEL // 2):
        a, b = 2 * p, 2 * p + 1
        out_ref[:, p * LANES : (p + 1) * LANES] = join_halves(
            recv_ref[owner_ref[a]], rank_ref[a], recv_ref[owner_ref[b]], rank_ref[b]
        )


def compact(owner, rank, recv):
    return pl.pallas_call(
        compact_kernel,
        out_shape=jax.ShapeDtypeStruct((FEAT, KEYS), jnp.bfloat16),
        in_specs=[
            pl.BlockSpec(memory_space=pltpu.SMEM),
            pl.BlockSpec(memory_space=pltpu.SMEM),
            pl.BlockSpec(memory_space=pltpu.VMEM),
        ],
        out_specs=pl.BlockSpec(memory_space=pltpu.VMEM),
        compiler_params=pltpu.CompilerParams(vmem_limit_bytes=16 * 2**20),
        cost_estimate=pl.CostEstimate(flops=0, bytes_accessed=2 * 2**20, transcendentals=0),
        name="compact",
    )(owner, rank, recv)


def attend_kernel(info_ref, pos_ref, q_ref, k0, k1, k2, k3, w_ref, out_ref, keys, sem):
    rows = q_ref.shape[0]

    @pl.when(pl.program_id(0) == 0)
    def _():
        copies = []
        for n, ref in enumerate((k0, k1, k2, k3)):
            part = lax.rem(info_ref[1] + XDIM - n, XDIM)
            place = pl.ds(pl.multiple_of(part * FEAT, 16), FEAT)
            copies.append(pltpu.make_async_copy(ref, keys.at[place, :], sem.at[n]))
        for copy in copies:
            copy.start()
        for copy in copies:
            copy.wait()

    tok = lax.broadcasted_iota(jnp.int32, (rows, 1), 0) % BLOCK
    query_pos = info_ref[0] + tok
    q = q_ref[...]
    width = 512
    scores = []
    for c in range(0, KEYS, width):
        s = jnp.dot(q, keys[:, c : c + width], preferred_element_type=jnp.float32)
        scores.append(jnp.where(pos_ref[:, c : c + width] <= query_pos, s, -jnp.inf))
    peak = jnp.max(functools.reduce(jnp.maximum, scores), axis=1, keepdims=True)
    total = jnp.zeros((rows, width), jnp.float32)
    acc = jnp.zeros((rows, LATENT), jnp.float32)
    for n, s in enumerate(scores):
        p = jnp.exp2((s - peak) * (SCALE * LOG2E))
        total = total + p
        acc = acc + lax.dot_general(
            p.astype(jnp.bfloat16),
            keys[:LATENT, n * width : (n + 1) * width],
            (((1,), (1,)), ((), ())),
            preferred_element_type=jnp.float32,
        )
    attended = (acc / jnp.sum(total, axis=1, keepdims=True)).astype(jnp.bfloat16)
    for n in range(rows // BLOCK):
        values = jnp.dot(attended[n * BLOCK : (n + 1) * BLOCK], w_ref[n], preferred_element_type=jnp.float32)
        out_ref[:, n * VHEAD : (n + 1) * VHEAD] = values.astype(jnp.bfloat16)


def attend(info, pos, q, chunks, w_uv):
    rows_all = q.shape[0]
    tile = 512
    heads = tile // BLOCK
    whole = pl.BlockSpec(memory_space=pl.ANY)
    return pl.pallas_call(
        attend_kernel,
        grid=(rows_all // tile,),
        out_shape=jax.ShapeDtypeStruct((BLOCK, rows_all // BLOCK * VHEAD), jnp.bfloat16),
        in_specs=[
            pl.BlockSpec(memory_space=pltpu.SMEM),
            pl.BlockSpec(pos.shape, lambda i: (0, 0)),
            pl.BlockSpec((tile, WIDTH), lambda i: (i, 0)),
            whole,
            whole,
            whole,
            whole,
            pl.BlockSpec((heads, LATENT, VHEAD), lambda i: (i, 0, 0)),
        ],
        out_specs=pl.BlockSpec((BLOCK, heads * VHEAD), lambda i: (0, i)),
        scratch_shapes=[pltpu.VMEM((WIDTH, KEYS), jnp.bfloat16), pltpu.SemaphoreType.DMA((XDIM,))],
        compiler_params=pltpu.CompilerParams(vmem_limit_bytes=32 * 2**20),
        cost_estimate=pl.CostEstimate(flops=5 * 10**9, bytes_accessed=8 * 2**20, transcendentals=2**21),
        name="attend",
    )(info, pos, q, *chunks, w_uv)


def project_kernel(info_ref, *refs):
    pieces, shards = refs[:GROUP], refs[GROUP : GROUP + ZDIM]
    own_ref, other_ref, rows, w, row_sem, w_sem = refs[GROUP + ZDIM :]
    x, y, z, core = (info_ref[n] for n in range(4))
    copies = []
    for n, ref in enumerate(pieces):
        for side in range(2):
            start = n * LANES + jnp.bitwise_xor(core, side) * BLOCK
            place = pl.ds(pl.multiple_of(start, BLOCK), BLOCK)
            copies.append(
                pltpu.make_async_copy(
                    ref.at[pl.ds(side * BLOCK, BLOCK), :], rows.at[place, :], row_sem.at[2 * n + side]
                )
            )
    for n, ref in enumerate(shards):
        for j in range(2):
            col = j * ZDIM * VHEAD + jnp.bitwise_and(z + n, ZDIM - 1) * VHEAD
            place = pl.ds(pl.multiple_of(col, VHEAD), VHEAD)
            copies.append(
                pltpu.make_async_copy(
                    ref.at[:, pl.ds(j * VHEAD, VHEAD)], w.at[:, place], w_sem.at[2 * n + j]
                )
            )
    for copy in copies:
        copy.start()
    for copy in copies:
        copy.wait()
    half = own_ref.shape[2]
    upper = lax.shift_right_logical(y, 1)
    for j in range(2):
        for side, out_ref in enumerate((own_ref, other_ref)):
            col = pl.multiple_of((2 * j + jnp.bitwise_xor(core, side)) * half, half)
            out = jnp.dot(rows[...], w[:, pl.ds(col, half)], preferred_element_type=jnp.float32)
            out = out.astype(jnp.bfloat16)
            for n in range(GROUP):
                to = jnp.bitwise_xor(2 * upper + j, 2 * n)
                out_ref[jnp.bitwise_and(to + XDIM - x, XDIM - 1)] = out[n * LANES : (n + 1) * LANES]


def project(info, pieces, shards):
    depth, cols = shards[0].shape
    count = GROUP * LANES
    return pl.pallas_call(
        project_kernel,
        in_specs=[pl.BlockSpec(memory_space=pltpu.SMEM)] + [pl.BlockSpec(memory_space=pl.ANY)] * (GROUP + ZDIM),
        out_specs=[pl.BlockSpec(memory_space=pltpu.VMEM)] * 2,
        out_shape=[jax.ShapeDtypeStruct((XDIM, LANES, ZDIM * cols // 4), jnp.bfloat16)] * 2,
        scratch_shapes=[
            pltpu.VMEM((count, depth), jnp.bfloat16),
            pltpu.VMEM((depth, ZDIM * cols), jnp.bfloat16),
            pltpu.SemaphoreType.DMA((2 * GROUP,)),
            pltpu.SemaphoreType.DMA((2 * ZDIM,)),
        ],
        compiler_params=pltpu.CompilerParams(vmem_limit_bytes=20 * 2**20),
        cost_estimate=pl.CostEstimate(flops=10**9, bytes_accessed=6 * 2**20, transcendentals=0),
        name="project",
    )(info, *pieces, *shards)


def per_device(queries, latents, selected, w_uv, w_out):
    n_ctx = lax.axis_size("ctx")
    n_head = lax.axis_size("head")
    shard = lax.axis_index("ctx")
    head = lax.axis_index("head")
    core = jnp.bitwise_and(head, 1)
    x = lax.shift_right_logical(head, 1)
    y = lax.shift_right_logical(shard, 3)
    z = jnp.bitwise_and(shard, ZDIM - 1)
    tok_dev, heads_here, width = queries.shape
    blocks_dev = latents.shape[0] // BLOCK
    first_block = blocks_dev * n_ctx - (tok_dev // BLOCK) * n_ctx
    swap = [(i, i ^ 1) for i in range(n_head)]

    def along_x(value, d):
        return lax.ppermute(value, "head", [(i, (i + 2 * d) % n_head) for i in range(n_head)])

    def along_y(value, d):
        return lax.ppermute(value, "ctx", [(i, (i + ZDIM * d) % n_ctx) for i in range(n_ctx)])

    def along_z(value, d):
        return lax.ppermute(value, "ctx", [(i, i // ZDIM * ZDIM + (i + d) % ZDIM) for i in range(n_ctx)])

    picks = jnp.where(core == 0, selected[0], selected[1])
    owner = lax.shift_right_logical(picks, 6)
    local = jnp.bitwise_and(picks, blocks_dev - 1)
    order = jnp.arange(SEL, dtype=jnp.int32)
    same = (owner[:, None] == owner[None, :]) & (order[None, :] < order[:, None])
    rank = jnp.sum(same.astype(jnp.int32), axis=1)
    slot = owner * PER_OWNER + rank
    match = slot[:, None, None] == (
        jnp.arange(n_ctx, dtype=jnp.int32)[None, :, None] * PER_OWNER
        + jnp.arange(LANES, dtype=jnp.int32)[None, None, :] // BLOCK
    )
    wanted = jnp.sum(jnp.where(match, local[:, None, None], 0), axis=0).astype(jnp.bfloat16)
    req = lax.all_to_all(wanted, "ctx", split_axis=0, concat_axis=0, tiled=True)
    req = req[:, ::BLOCK].astype(jnp.int32).reshape(-1)

    slab = lax.dynamic_slice_in_dim(latents.T, x * FEAT, FEAT, axis=0)
    up1, down1 = along_z(w_out, 1), along_z(w_out, -1)
    req, near, up1, down1 = lax.optimization_barrier((req, w_out, up1, down1))

    def peer_of(own):
        return lax.ppermute(own, "ctx", [(i, i ^ ZDIM) for i in range(n_ctx)])

    def pair(own, peer):
        even = jnp.bitwise_and(y, 1) == 0
        return jnp.where(even, jnp.concatenate([own, peer], axis=1), jnp.concatenate([peer, own], axis=1))

    piece = gather_rows(req, slab, n_ctx)
    recv = lax.all_to_all(piece, "ctx", split_axis=0, concat_axis=0, tiled=True)

    by_head = queries.transpose(1, 0, 2)
    mine = lax.dynamic_slice_in_dim(by_head, core * BLOCK, BLOCK, axis=1)
    theirs = lax.dynamic_slice_in_dim(by_head, (1 - core) * BLOCK, BLOCK, axis=1)
    got = lax.ppermute(theirs, "head", swap)
    uv_other = lax.ppermute(w_uv, "head", swap)
    q = jnp.concatenate([mine, got], axis=0).reshape(2 * heads_here * BLOCK, width)
    uv_pair = jnp.concatenate([w_uv, uv_other], axis=0)

    chunk = compact(owner, rank, recv)
    up1, down1 = pair(up1, peer_of(up1)), pair(down1, peer_of(down1))
    chunk, up1, down1 = lax.optimization_barrier((chunk, up1, down1))
    chunks = [chunk] + [along_x(chunk, d) for d in range(1, XDIM)]
    up2, down2 = along_z(up1, 1), along_z(down1, -1)
    up3, down3 = along_z(up2, 1), along_z(down2, -1)
    chunks[3], near, up3, down3 = lax.optimization_barrier((chunks[3], near, up3, down3))
    w_peer = peer_of(near)
    up4 = along_z(up3, 1)
    pos = (picks[:, None] * BLOCK + jnp.arange(BLOCK, dtype=jnp.int32)[None, :]).reshape(1, -1)
    first = (first_block + shard * (tok_dev // BLOCK) + core) * BLOCK
    values = attend(jnp.stack([first, x]), pos, q, chunks, uv_pair)

    values, w_peer = lax.optimization_barrier((values, w_peer))
    w_pair = pair(near, w_peer)
    half = heads_here * VHEAD
    values = jnp.concatenate([values[:, :half], lax.ppermute(values[:, half:], "head", swap)], axis=0)
    pieces = [values, along_y(values, 2)]
    info = jnp.stack([x, y, z, core])
    kept, sent = project(info, pieces, [w_pair, down1, down2, down3, up4, up3, up2, up1])
    other = lax.ppermute(sent, "head", swap)
    both = (kept.astype(jnp.float32) + other.astype(jnp.float32)).astype(jnp.bfloat16)
    total = both[0].astype(jnp.float32)
    for d in range(1, XDIM):
        total = total + along_x(both[d], d).astype(jnp.float32)
    total = total.astype(jnp.bfloat16)
    route = []
    for c in range(n_ctx):
        for h in range(n_head):
            if c // (2 * ZDIM) != h // 4:
                route.append((c * n_head + h, (c ^ (2 * ZDIM)) * n_head + (h ^ 4)))
    moved = lax.ppermute(total, ("ctx", "head"), route)
    return jnp.where(lax.shift_right_logical(y, 1) == lax.shift_right_logical(x, 1), total, moved)


def solution(mesh):
    return jax.shard_map(
        per_device,
        mesh=mesh,
        in_specs=(
            P("ctx", "head", None),
            P("ctx", None),
            P("ctx", None),
            P("head", None, None),
            P("head", "ctx"),
        ),
        out_specs=P("ctx", "head"),
        check_vma=False,
    )
```

```python
import functools

import jax
import jax.numpy as jnp
from jax import lax
from jax.experimental import pallas as pl
from jax.experimental.pallas import tpu as pltpu
from jax.sharding import PartitionSpec as P

LATENT = 512
ROPE = 64
WIDTH = LATENT + ROPE
VHEAD = 128
BLOCK = 64
SEL = 32
KEYS = SEL * BLOCK
PER_OWNER = 2
XDIM = 4
YDIM = 4
GROUP = 2
ZDIM = 8
FEAT = WIDTH // XDIM
LANES = 2 * BLOCK
SCALE = 192.0 ** (-0.5)
LOG2E = 1.4426950408889634


def join_halves(a, a_half, b, b_half):
    lane = lax.broadcasted_iota(jnp.int32, a.shape, 1)
    low = pltpu.roll(a.astype(jnp.float32), a_half * BLOCK, 1)
    high = pltpu.roll(b.astype(jnp.float32), (1 - b_half) * BLOCK, 1)
    return jnp.where(lane < BLOCK, low, high).astype(a.dtype)


def gather_kernel(req_ref, slab_ref, out_ref):
    def pack(i, carry):
        pieces = []
        for side in range(2):
            block = req_ref[2 * i + side]
            col = pl.multiple_of(lax.shift_right_logical(block, 1) * LANES, LANES)
            pieces += [slab_ref[:, pl.ds(col, LANES)], jnp.bitwise_and(block, 1)]
        out_ref[i] = join_halves(*pieces)
        return carry

    lax.fori_loop(0, out_ref.shape[0], pack, 0, unroll=8)


def gather_rows(req, slab, n_ctx):
    return pl.pallas_call(
        gather_kernel,
        out_shape=jax.ShapeDtypeStruct((n_ctx, FEAT, LANES), jnp.bfloat16),
        in_specs=[
            pl.BlockSpec(memory_space=pltpu.SMEM),
            pl.BlockSpec(memory_space=pltpu.VMEM),
        ],
        out_specs=pl.BlockSpec(memory_space=pltpu.VMEM),
        compiler_params=pltpu.CompilerParams(vmem_limit_bytes=16 * 2**20),
        cost_estimate=pl.CostEstimate(flops=0, bytes_accessed=4 * 2**20, transcendentals=0),
        name="gather_rows",
    )(req, slab)


def compact_kernel(owner_ref, rank_ref, recv_ref, out_ref):
    for p in range(SEL // 2):
        a, b = 2 * p, 2 * p + 1
        out_ref[:, p * LANES : (p + 1) * LANES] = join_halves(
            recv_ref[owner_ref[a]], rank_ref[a], recv_ref[owner_ref[b]], rank_ref[b]
        )


def compact(owner, rank, recv):
    return pl.pallas_call(
        compact_kernel,
        out_shape=jax.ShapeDtypeStruct((FEAT, KEYS), jnp.bfloat16),
        in_specs=[
            pl.BlockSpec(memory_space=pltpu.SMEM),
            pl.BlockSpec(memory_space=pltpu.SMEM),
            pl.BlockSpec(memory_space=pltpu.VMEM),
        ],
        out_specs=pl.BlockSpec(memory_space=pltpu.VMEM),
        compiler_params=pltpu.CompilerParams(vmem_limit_bytes=16 * 2**20),
        cost_estimate=pl.CostEstimate(flops=0, bytes_accessed=2 * 2**20, transcendentals=0),
        name="compact",
    )(owner, rank, recv)


def attend_kernel(info_ref, pos_ref, q_ref, k0, k1, k2, k3, w_ref, out_ref, keys, sem):
    rows = q_ref.shape[0]

    @pl.when(pl.program_id(0) == 0)
    def _():
        copies = []
        for n, ref in enumerate((k0, k1, k2, k3)):
            part = lax.rem(info_ref[1] + XDIM - n, XDIM)
            place = pl.ds(pl.multiple_of(part * FEAT, 16), FEAT)
            copies.append(pltpu.make_async_copy(ref, keys.at[place, :], sem.at[n]))
        for copy in copies:
            copy.start()
        for copy in copies:
            copy.wait()

    tok = lax.broadcasted_iota(jnp.int32, (rows, 1), 0) % BLOCK
    query_pos = info_ref[0] + tok
    q = q_ref[...]
    width = 512
    scores = []
    for c in range(0, KEYS, width):
        s = jnp.dot(q, keys[:, c : c + width], preferred_element_type=jnp.float32)
        scores.append(jnp.where(pos_ref[:, c : c + width] <= query_pos, s, -jnp.inf))
    peak = jnp.max(functools.reduce(jnp.maximum, scores), axis=1, keepdims=True)
    total = jnp.zeros((rows, width), jnp.float32)
    acc = jnp.zeros((rows, LATENT), jnp.float32)
    for n, s in enumerate(scores):
        p = jnp.exp2((s - peak) * (SCALE * LOG2E))
        total = total + p
        acc = acc + lax.dot_general(
            p.astype(jnp.bfloat16),
            keys[:LATENT, n * width : (n + 1) * width],
            (((1,), (1,)), ((), ())),
            preferred_element_type=jnp.float32,
        )
    attended = (acc / jnp.sum(total, axis=1, keepdims=True)).astype(jnp.bfloat16)
    for n in range(rows // BLOCK):
        values = jnp.dot(attended[n * BLOCK : (n + 1) * BLOCK], w_ref[n], preferred_element_type=jnp.float32)
        out_ref[:, n * VHEAD : (n + 1) * VHEAD] = values.astype(jnp.bfloat16)


def attend(info, pos, q, chunks, w_uv):
    rows_all = q.shape[0]
    tile = 512
    heads = tile // BLOCK
    whole = pl.BlockSpec(memory_space=pl.ANY)
    return pl.pallas_call(
        attend_kernel,
        grid=(rows_all // tile,),
        out_shape=jax.ShapeDtypeStruct((BLOCK, rows_all // BLOCK * VHEAD), jnp.bfloat16),
        in_specs=[
            pl.BlockSpec(memory_space=pltpu.SMEM),
            pl.BlockSpec(pos.shape, lambda i: (0, 0)),
            pl.BlockSpec((tile, WIDTH), lambda i: (i, 0)),
            whole,
            whole,
            whole,
            whole,
            pl.BlockSpec((heads, LATENT, VHEAD), lambda i: (i, 0, 0)),
        ],
        out_specs=pl.BlockSpec((BLOCK, heads * VHEAD), lambda i: (0, i)),
        scratch_shapes=[pltpu.VMEM((WIDTH, KEYS), jnp.bfloat16), pltpu.SemaphoreType.DMA((XDIM,))],
        compiler_params=pltpu.CompilerParams(vmem_limit_bytes=32 * 2**20),
        cost_estimate=pl.CostEstimate(flops=5 * 10**9, bytes_accessed=8 * 2**20, transcendentals=2**21),
        name="attend",
    )(info, pos, q, *chunks, w_uv)


def project_kernel(info_ref, *refs):
    pieces, shards = refs[: 2 * GROUP], refs[2 * GROUP : 2 * GROUP + ZDIM]
    own_ref, other_ref, rows, w, row_sem, w_sem = refs[2 * GROUP + ZDIM :]
    x, y, z, core = (info_ref[n] for n in range(4))
    copies = []
    for n, ref in enumerate(pieces):
        start = n // 2 * LANES + jnp.bitwise_xor(core, n % 2) * BLOCK
        place = pl.ds(pl.multiple_of(start, BLOCK), BLOCK)
        copies.append(pltpu.make_async_copy(ref, rows.at[place, :], row_sem.at[n]))
    for n, ref in enumerate(shards):
        for j in range(2):
            col = j * ZDIM * VHEAD + jnp.bitwise_and(z + n, ZDIM - 1) * VHEAD
            place = pl.ds(pl.multiple_of(col, VHEAD), VHEAD)
            copies.append(
                pltpu.make_async_copy(
                    ref.at[:, pl.ds(j * VHEAD, VHEAD)], w.at[:, place], w_sem.at[2 * n + j]
                )
            )
    for copy in copies:
        copy.start()
    for copy in copies:
        copy.wait()
    half = own_ref.shape[2]
    upper = lax.shift_right_logical(y, 1)
    for j in range(2):
        for side, out_ref in enumerate((own_ref, other_ref)):
            col = pl.multiple_of((2 * j + jnp.bitwise_xor(core, side)) * half, half)
            out = jnp.dot(rows[...], w[:, pl.ds(col, half)], preferred_element_type=jnp.float32)
            out = out.astype(jnp.bfloat16)
            for n in range(GROUP):
                to = jnp.bitwise_xor(2 * upper + j, 2 * n)
                out_ref[jnp.bitwise_and(to + XDIM - x, XDIM - 1)] = out[n * LANES : (n + 1) * LANES]


def project(info, pieces, shards):
    depth, cols = shards[0].shape
    count = GROUP * LANES
    return pl.pallas_call(
        project_kernel,
        in_specs=[pl.BlockSpec(memory_space=pltpu.SMEM)] + [pl.BlockSpec(memory_space=pl.ANY)] * (2 * GROUP + ZDIM),
        out_specs=[pl.BlockSpec(memory_space=pltpu.VMEM)] * 2,
        out_shape=[jax.ShapeDtypeStruct((XDIM, LANES, ZDIM * cols // 4), jnp.bfloat16)] * 2,
        scratch_shapes=[
            pltpu.VMEM((count, depth), jnp.bfloat16),
            pltpu.VMEM((depth, ZDIM * cols), jnp.bfloat16),
            pltpu.SemaphoreType.DMA((2 * GROUP,)),
            pltpu.SemaphoreType.DMA((2 * ZDIM,)),
        ],
        compiler_params=pltpu.CompilerParams(vmem_limit_bytes=20 * 2**20),
        cost_estimate=pl.CostEstimate(flops=10**9, bytes_accessed=6 * 2**20, transcendentals=0),
        name="project",
    )(info, *pieces, *shards)


def per_device(queries, latents, selected, w_uv, w_out):
    n_ctx = lax.axis_size("ctx")
    n_head = lax.axis_size("head")
    shard = lax.axis_index("ctx")
    head = lax.axis_index("head")
    core = jnp.bitwise_and(head, 1)
    x = lax.shift_right_logical(head, 1)
    y = lax.shift_right_logical(shard, 3)
    z = jnp.bitwise_and(shard, ZDIM - 1)
    tok_dev, heads_here, width = queries.shape
    blocks_dev = latents.shape[0] // BLOCK
    first_block = blocks_dev * n_ctx - (tok_dev // BLOCK) * n_ctx
    swap = [(i, i ^ 1) for i in range(n_head)]

    def along_x(value, d):
        return lax.ppermute(value, "head", [(i, (i + 2 * d) % n_head) for i in range(n_head)])

    def along_y(value, d):
        return lax.ppermute(value, "ctx", [(i, (i + ZDIM * d) % n_ctx) for i in range(n_ctx)])

    def along_z(value, d):
        return lax.ppermute(value, "ctx", [(i, i // ZDIM * ZDIM + (i + d) % ZDIM) for i in range(n_ctx)])

    picks = jnp.where(core == 0, selected[0], selected[1])
    owner = lax.shift_right_logical(picks, 6)
    local = jnp.bitwise_and(picks, blocks_dev - 1)
    order = jnp.arange(SEL, dtype=jnp.int32)
    same = (owner[:, None] == owner[None, :]) & (order[None, :] < order[:, None])
    rank = jnp.sum(same.astype(jnp.int32), axis=1)
    slot = owner * PER_OWNER + rank
    match = slot[:, None, None] == (
        jnp.arange(n_ctx, dtype=jnp.int32)[None, :, None] * PER_OWNER
        + jnp.arange(LANES, dtype=jnp.int32)[None, None, :] // BLOCK
    )
    wanted = jnp.sum(jnp.where(match, local[:, None, None], 0), axis=0).astype(jnp.bfloat16)
    req = lax.all_to_all(wanted, "ctx", split_axis=0, concat_axis=0, tiled=True)
    req = req[:, ::BLOCK].astype(jnp.int32).reshape(-1)

    slab = lax.dynamic_slice_in_dim(latents.T, x * FEAT, FEAT, axis=0)
    up1, down1 = along_z(w_out, 1), along_z(w_out, -1)
    req, near, up1, down1 = lax.optimization_barrier((req, w_out, up1, down1))

    def peer_of(own):
        return lax.ppermute(own, "ctx", [(i, i ^ ZDIM) for i in range(n_ctx)])

    def pair(own, peer):
        even = jnp.bitwise_and(y, 1) == 0
        return jnp.where(even, jnp.concatenate([own, peer], axis=1), jnp.concatenate([peer, own], axis=1))

    piece = gather_rows(req, slab, n_ctx)
    recv = lax.all_to_all(piece, "ctx", split_axis=0, concat_axis=0, tiled=True)

    by_head = queries.transpose(1, 0, 2)
    mine = lax.dynamic_slice_in_dim(by_head, core * BLOCK, BLOCK, axis=1)
    theirs = lax.dynamic_slice_in_dim(by_head, (1 - core) * BLOCK, BLOCK, axis=1)
    got = lax.ppermute(theirs, "head", swap)
    uv_other = lax.ppermute(w_uv, "head", swap)
    q = jnp.concatenate([mine, got], axis=0).reshape(2 * heads_here * BLOCK, width)
    uv_pair = jnp.concatenate([w_uv, uv_other], axis=0)

    chunk = compact(owner, rank, recv)
    up1, down1 = pair(up1, peer_of(up1)), pair(down1, peer_of(down1))
    chunk, up1, down1 = lax.optimization_barrier((chunk, up1, down1))
    chunks = [chunk] + [along_x(chunk, d) for d in range(1, XDIM)]
    up2, down2 = along_z(up1, 1), along_z(down1, -1)
    up3, down3 = along_z(up2, 1), along_z(down2, -1)
    chunks[3], near, up3, down3 = lax.optimization_barrier((chunks[3], near, up3, down3))
    w_peer = peer_of(near)
    up4 = along_z(up3, 1)
    pos = (picks[:, None] * BLOCK + jnp.arange(BLOCK, dtype=jnp.int32)[None, :]).reshape(1, -1)
    first = (first_block + shard * (tok_dev // BLOCK) + core) * BLOCK
    values = attend(jnp.stack([first, x]), pos, q, chunks, uv_pair)

    values, w_peer = lax.optimization_barrier((values, w_peer))
    w_pair = pair(near, w_peer)
    half = heads_here * VHEAD
    own, swapped = values[:, :half], lax.ppermute(values[:, half:], "head", swap)
    pieces = [own, swapped, along_y(own, 2), along_y(swapped, 2)]
    info = jnp.stack([x, y, z, core])
    kept, sent = project(info, pieces, [w_pair, down1, down2, down3, up4, up3, up2, up1])
    other = lax.ppermute(sent, "head", swap)
    both = (kept.astype(jnp.float32) + other.astype(jnp.float32)).astype(jnp.bfloat16)
    total = both[0].astype(jnp.float32)
    for d in range(1, XDIM):
        total = total + along_x(both[d], d).astype(jnp.float32)
    total = total.astype(jnp.bfloat16)
    route = []
    for c in range(n_ctx):
        for h in range(n_head):
            if c // (2 * ZDIM) != h // 4:
                route.append((c * n_head + h, (c ^ (2 * ZDIM)) * n_head + (h ^ 4)))
    moved = lax.ppermute(total, ("ctx", "head"), route)
    return jnp.where(lax.shift_right_logical(y, 1) == lax.shift_right_logical(x, 1), total, moved)


def solution(mesh):
    return jax.shard_map(
        per_device,
        mesh=mesh,
        in_specs=(
            P("ctx", "head", None),
            P("ctx", None),
            P("ctx", None),
            P("head", None, None),
            P("head", "ctx"),
        ),
        out_specs=P("ctx", "head"),
        check_vma=False,
    )
```

```python
import functools

import jax
import jax.numpy as jnp
from jax import lax
from jax.experimental import pallas as pl
from jax.experimental.pallas import tpu as pltpu
from jax.sharding import PartitionSpec as P

LATENT = 512
ROPE = 64
WIDTH = LATENT + ROPE
VHEAD = 128
BLOCK = 64
SEL = 32
KEYS = SEL * BLOCK
PER_OWNER = 2
XDIM = 4
YDIM = 4
GROUP = 2
ZDIM = 8
FEAT = WIDTH // XDIM
LANES = 2 * BLOCK
SCALE = 192.0 ** (-0.5)
LOG2E = 1.4426950408889634


def join_halves(a, a_half, b, b_half):
    lane = lax.broadcasted_iota(jnp.int32, a.shape, 1)
    low = pltpu.roll(a.astype(jnp.float32), a_half * BLOCK, 1)
    high = pltpu.roll(b.astype(jnp.float32), (1 - b_half) * BLOCK, 1)
    return jnp.where(lane < BLOCK, low, high).astype(a.dtype)


def gather_kernel(req_ref, slab_ref, out_ref):
    def pack(i, carry):
        pieces = []
        for side in range(2):
            block = req_ref[2 * i + side]
            col = pl.multiple_of(lax.shift_right_logical(block, 1) * LANES, LANES)
            pieces += [slab_ref[:, pl.ds(col, LANES)], jnp.bitwise_and(block, 1)]
        out_ref[i] = join_halves(*pieces)
        return carry

    lax.fori_loop(0, out_ref.shape[0], pack, 0, unroll=8)


def gather_rows(req, slab, n_ctx):
    return pl.pallas_call(
        gather_kernel,
        out_shape=jax.ShapeDtypeStruct((n_ctx, FEAT, LANES), jnp.bfloat16),
        in_specs=[
            pl.BlockSpec(memory_space=pltpu.SMEM),
            pl.BlockSpec(memory_space=pltpu.VMEM),
        ],
        out_specs=pl.BlockSpec(memory_space=pltpu.VMEM),
        compiler_params=pltpu.CompilerParams(vmem_limit_bytes=16 * 2**20),
        cost_estimate=pl.CostEstimate(flops=0, bytes_accessed=4 * 2**20, transcendentals=0),
        name="gather_rows",
    )(req, slab)


def compact_kernel(owner_ref, rank_ref, recv_ref, out_ref):
    for p in range(SEL // 2):
        a, b = 2 * p, 2 * p + 1
        out_ref[:, p * LANES : (p + 1) * LANES] = join_halves(
            recv_ref[owner_ref[a]], rank_ref[a], recv_ref[owner_ref[b]], rank_ref[b]
        )


def compact(owner, rank, recv):
    return pl.pallas_call(
        compact_kernel,
        out_shape=jax.ShapeDtypeStruct((FEAT, KEYS), jnp.bfloat16),
        in_specs=[
            pl.BlockSpec(memory_space=pltpu.SMEM),
            pl.BlockSpec(memory_space=pltpu.SMEM),
            pl.BlockSpec(memory_space=pltpu.VMEM),
        ],
        out_specs=pl.BlockSpec(memory_space=pltpu.VMEM),
        compiler_params=pltpu.CompilerParams(vmem_limit_bytes=16 * 2**20),
        cost_estimate=pl.CostEstimate(flops=0, bytes_accessed=2 * 2**20, transcendentals=0),
        name="compact",
    )(owner, rank, recv)


def attend_kernel(info_ref, pos_ref, q_ref, k0, k1, k2, k3, w_ref, out_ref, keys, sem):
    rows = q_ref.shape[0]

    @pl.when(pl.program_id(0) == 0)
    def _():
        copies = []
        for n, ref in enumerate((k0, k1, k2, k3)):
            part = lax.rem(info_ref[1] + XDIM - n, XDIM)
            place = pl.ds(pl.multiple_of(part * FEAT, 16), FEAT)
            copies.append(pltpu.make_async_copy(ref, keys.at[place, :], sem.at[n]))
        for copy in copies:
            copy.start()
        for copy in copies:
            copy.wait()

    tok = lax.broadcasted_iota(jnp.int32, (rows, 1), 0) % BLOCK
    query_pos = info_ref[0] + tok
    q = q_ref[...]
    width = 512
    scores = []
    for c in range(0, KEYS, width):
        s = jnp.dot(q, keys[:, c : c + width], preferred_element_type=jnp.float32)
        scores.append(jnp.where(pos_ref[:, c : c + width] <= query_pos, s, -jnp.inf))
    peak = jnp.max(functools.reduce(jnp.maximum, scores), axis=1, keepdims=True)
    total = jnp.zeros((rows, width), jnp.float32)
    acc = jnp.zeros((rows, LATENT), jnp.float32)
    for n, s in enumerate(scores):
        p = jnp.exp2((s - peak) * (SCALE * LOG2E))
        total = total + p
        acc = acc + lax.dot_general(
            p.astype(jnp.bfloat16),
            keys[:LATENT, n * width : (n + 1) * width],
            (((1,), (1,)), ((), ())),
            preferred_element_type=jnp.float32,
        )
    attended = (acc / jnp.sum(total, axis=1, keepdims=True)).astype(jnp.bfloat16)
    for n in range(rows // BLOCK):
        values = jnp.dot(attended[n * BLOCK : (n + 1) * BLOCK], w_ref[n], preferred_element_type=jnp.float32)
        out_ref[:, n * VHEAD : (n + 1) * VHEAD] = values.astype(jnp.bfloat16)


def attend(info, pos, q, chunks, w_uv):
    rows_all = q.shape[0]
    tile = 512
    heads = tile // BLOCK
    whole = pl.BlockSpec(memory_space=pl.ANY)
    return pl.pallas_call(
        attend_kernel,
        grid=(rows_all // tile,),
        out_shape=jax.ShapeDtypeStruct((BLOCK, rows_all // BLOCK * VHEAD), jnp.bfloat16),
        in_specs=[
            pl.BlockSpec(memory_space=pltpu.SMEM),
            pl.BlockSpec(pos.shape, lambda i: (0, 0)),
            pl.BlockSpec((tile, WIDTH), lambda i: (i, 0)),
            whole,
            whole,
            whole,
            whole,
            pl.BlockSpec((heads, LATENT, VHEAD), lambda i: (i, 0, 0)),
        ],
        out_specs=pl.BlockSpec((BLOCK, heads * VHEAD), lambda i: (0, i)),
        scratch_shapes=[pltpu.VMEM((WIDTH, KEYS), jnp.bfloat16), pltpu.SemaphoreType.DMA((XDIM,))],
        compiler_params=pltpu.CompilerParams(vmem_limit_bytes=32 * 2**20),
        cost_estimate=pl.CostEstimate(flops=5 * 10**9, bytes_accessed=8 * 2**20, transcendentals=2**21),
        name="attend",
    )(info, pos, q, *chunks, w_uv)


def project_kernel(info_ref, *refs):
    pieces, shards = refs[: 2 * GROUP], refs[2 * GROUP : 2 * GROUP + ZDIM]
    own_ref, other_ref, rows, w, row_sem, w_sem = refs[2 * GROUP + ZDIM :]
    x, y, z, core = (info_ref[n] for n in range(4))
    copies = []
    for n, ref in enumerate(pieces):
        start = n // 2 * LANES + jnp.bitwise_xor(core, n % 2) * BLOCK
        place = pl.ds(pl.multiple_of(start, BLOCK), BLOCK)
        copies.append(pltpu.make_async_copy(ref, rows.at[place, :], row_sem.at[n]))
    for n, ref in enumerate(shards):
        for j in range(2):
            col = j * ZDIM * VHEAD + jnp.bitwise_and(z + n, ZDIM - 1) * VHEAD
            place = pl.ds(pl.multiple_of(col, VHEAD), VHEAD)
            copies.append(
                pltpu.make_async_copy(
                    ref.at[:, pl.ds(j * VHEAD, VHEAD)], w.at[:, place], w_sem.at[2 * n + j]
                )
            )
    for copy in copies:
        copy.start()
    for copy in copies:
        copy.wait()
    half = own_ref.shape[2]
    upper = lax.shift_right_logical(y, 1)
    for j in range(2):
        for side, out_ref in enumerate((own_ref, other_ref)):
            col = pl.multiple_of((2 * j + jnp.bitwise_xor(core, side)) * half, half)
            out = jnp.dot(rows[...], w[:, pl.ds(col, half)], preferred_element_type=jnp.float32)
            out = out.astype(jnp.bfloat16)
            for n in range(GROUP):
                to = jnp.bitwise_xor(2 * upper + j, 2 * n)
                out_ref[jnp.bitwise_and(to + XDIM - x, XDIM - 1)] = out[n * LANES : (n + 1) * LANES]


def project(info, pieces, shards):
    depth, cols = shards[0].shape
    count = GROUP * LANES
    return pl.pallas_call(
        project_kernel,
        in_specs=[pl.BlockSpec(memory_space=pltpu.SMEM)] + [pl.BlockSpec(memory_space=pl.ANY)] * (2 * GROUP + ZDIM),
        out_specs=[pl.BlockSpec(memory_space=pltpu.VMEM)] * 2,
        out_shape=[jax.ShapeDtypeStruct((XDIM, LANES, ZDIM * cols // 4), jnp.bfloat16)] * 2,
        scratch_shapes=[
            pltpu.VMEM((count, depth), jnp.bfloat16),
            pltpu.VMEM((depth, ZDIM * cols), jnp.bfloat16),
            pltpu.SemaphoreType.DMA((2 * GROUP,)),
            pltpu.SemaphoreType.DMA((2 * ZDIM,)),
        ],
        compiler_params=pltpu.CompilerParams(vmem_limit_bytes=20 * 2**20),
        cost_estimate=pl.CostEstimate(flops=10**9, bytes_accessed=6 * 2**20, transcendentals=0),
        name="project",
    )(info, *pieces, *shards)


def per_device(queries, latents, selected, w_uv, w_out):
    n_ctx = lax.axis_size("ctx")
    n_head = lax.axis_size("head")
    shard = lax.axis_index("ctx")
    head = lax.axis_index("head")
    core = jnp.bitwise_and(head, 1)
    x = lax.shift_right_logical(head, 1)
    y = lax.shift_right_logical(shard, 3)
    z = jnp.bitwise_and(shard, ZDIM - 1)
    tok_dev, heads_here, width = queries.shape
    blocks_dev = latents.shape[0] // BLOCK
    first_block = blocks_dev * n_ctx - (tok_dev // BLOCK) * n_ctx
    swap = [(i, i ^ 1) for i in range(n_head)]

    def along_x(value, d):
        return lax.ppermute(value, "head", [(i, (i + 2 * d) % n_head) for i in range(n_head)])

    def along_y(value, d):
        return lax.ppermute(value, "ctx", [(i, (i + ZDIM * d) % n_ctx) for i in range(n_ctx)])

    def along_z(value, d):
        return lax.ppermute(value, "ctx", [(i, i // ZDIM * ZDIM + (i + d) % ZDIM) for i in range(n_ctx)])

    picks = jnp.where(core == 0, selected[0], selected[1])
    owner = lax.shift_right_logical(picks, 6)
    local = jnp.bitwise_and(picks, blocks_dev - 1)
    order = jnp.arange(SEL, dtype=jnp.int32)
    same = (owner[:, None] == owner[None, :]) & (order[None, :] < order[:, None])
    rank = jnp.sum(same.astype(jnp.int32), axis=1)
    slot = owner * PER_OWNER + rank
    match = slot[:, None, None] == (
        jnp.arange(n_ctx, dtype=jnp.int32)[None, :, None] * PER_OWNER
        + jnp.arange(LANES, dtype=jnp.int32)[None, None, :] // BLOCK
    )
    wanted = jnp.sum(jnp.where(match, local[:, None, None], 0), axis=0).astype(jnp.bfloat16)
    req = lax.all_to_all(wanted, "ctx", split_axis=0, concat_axis=0, tiled=True)
    req = req[:, ::BLOCK].astype(jnp.int32).reshape(-1)

    slab = lax.dynamic_slice_in_dim(latents.T, x * FEAT, FEAT, axis=0)
    up1, down1 = along_z(w_out, 1), along_z(w_out, -1)
    req, near, up1, down1 = lax.optimization_barrier((req, w_out, up1, down1))

    def peer_of(own):
        return lax.ppermute(own, "ctx", [(i, i ^ ZDIM) for i in range(n_ctx)])

    def pair(own, peer):
        even = jnp.bitwise_and(y, 1) == 0
        return jnp.where(even, jnp.concatenate([own, peer], axis=1), jnp.concatenate([peer, own], axis=1))

    piece = gather_rows(req, slab, n_ctx)
    recv = lax.all_to_all(piece, "ctx", split_axis=0, concat_axis=0, tiled=True)

    by_head = queries.transpose(1, 0, 2)
    mine = lax.dynamic_slice_in_dim(by_head, core * BLOCK, BLOCK, axis=1)
    theirs = lax.dynamic_slice_in_dim(by_head, (1 - core) * BLOCK, BLOCK, axis=1)
    got = lax.ppermute(theirs, "head", swap)
    uv_other = lax.ppermute(w_uv, "head", swap)
    q = jnp.concatenate([mine, got], axis=0).reshape(2 * heads_here * BLOCK, width)
    uv_pair = jnp.concatenate([w_uv, uv_other], axis=0)

    chunk = compact(owner, rank, recv)
    up1, down1 = pair(up1, peer_of(up1)), pair(down1, peer_of(down1))
    chunk, up1, down1 = lax.optimization_barrier((chunk, up1, down1))
    chunks = [chunk] + [along_x(chunk, d) for d in range(1, XDIM)]
    up2, down2 = along_z(up1, 1), along_z(down1, -1)
    up3, down3 = along_z(up2, 1), along_z(down2, -1)
    chunks[3], near, up3, down3 = lax.optimization_barrier((chunks[3], near, up3, down3))
    w_peer = peer_of(near)
    up4 = along_z(up3, 1)
    pos = (picks[:, None] * BLOCK + jnp.arange(BLOCK, dtype=jnp.int32)[None, :]).reshape(1, -1)
    first = (first_block + shard * (tok_dev // BLOCK) + core) * BLOCK
    values = attend(jnp.stack([first, x]), pos, q, chunks, uv_pair)

    values, w_peer = lax.optimization_barrier((values, w_peer))
    w_pair = pair(near, w_peer)
    half = heads_here * VHEAD
    own, swapped = values[:, :half], lax.ppermute(values[:, half:], "head", swap)
    pieces = [own, swapped, along_y(own, 2), along_y(swapped, 2)]
    info = jnp.stack([x, y, z, core])
    kept, sent = project(info, pieces, [w_pair, down1, down2, down3, up4, up3, up2, up1])
    other = lax.ppermute(sent, "head", swap)
    both = (kept.astype(jnp.float32) + other.astype(jnp.float32)).astype(jnp.bfloat16)
    total = jnp.zeros(both.shape[1:], jnp.float32)
    for d in range(XDIM):
        route = []
        for c in range(n_ctx):
            for h in range(n_head):
                to = (h + 2 * d) % n_head
                foreign = c // (2 * ZDIM) != to // 4
                route.append((c * n_head + h, (c ^ (2 * ZDIM)) * n_head + (to ^ 4) if foreign else c * n_head + to))
        total = total + lax.ppermute(both[d], ("ctx", "head"), route).astype(jnp.float32)
    return total.astype(jnp.bfloat16)


def solution(mesh):
    return jax.shard_map(
        per_device,
        mesh=mesh,
        in_specs=(
            P("ctx", "head", None),
            P("ctx", None),
            P("ctx", None),
            P("head", None, None),
            P("head", "ctx"),
        ),
        out_specs=P("ctx", "head"),
        check_vma=False,
    )
```

```python
import functools

import jax
import jax.numpy as jnp
from jax import lax
from jax.experimental import pallas as pl
from jax.experimental.pallas import tpu as pltpu
from jax.sharding import PartitionSpec as P

LATENT = 512
ROPE = 64
WIDTH = LATENT + ROPE
VHEAD = 128
BLOCK = 64
SEL = 32
KEYS = SEL * BLOCK
PER_OWNER = 2
XDIM = 4
YDIM = 4
GROUP = 2
ZDIM = 8
FEAT = WIDTH // XDIM
LANES = 2 * BLOCK
SCALE = 192.0 ** (-0.5)
LOG2E = 1.4426950408889634


def join_halves(a, a_half, b, b_half):
    lane = lax.broadcasted_iota(jnp.int32, a.shape, 1)
    low = pltpu.roll(a.astype(jnp.float32), a_half * BLOCK, 1)
    high = pltpu.roll(b.astype(jnp.float32), (1 - b_half) * BLOCK, 1)
    return jnp.where(lane < BLOCK, low, high).astype(a.dtype)


def gather_kernel(req_ref, slab_ref, out_ref):
    def pack(i, carry):
        pieces = []
        for side in range(2):
            block = req_ref[2 * i + side]
            col = pl.multiple_of(lax.shift_right_logical(block, 1) * LANES, LANES)
            pieces += [slab_ref[:, pl.ds(col, LANES)], jnp.bitwise_and(block, 1)]
        out_ref[i] = join_halves(*pieces)
        return carry

    lax.fori_loop(0, out_ref.shape[0], pack, 0, unroll=8)


def gather_rows(req, slab, n_ctx):
    return pl.pallas_call(
        gather_kernel,
        out_shape=jax.ShapeDtypeStruct((n_ctx, FEAT, LANES), jnp.bfloat16),
        in_specs=[
            pl.BlockSpec(memory_space=pltpu.SMEM),
            pl.BlockSpec(memory_space=pltpu.VMEM),
        ],
        out_specs=pl.BlockSpec(memory_space=pltpu.VMEM),
        compiler_params=pltpu.CompilerParams(vmem_limit_bytes=16 * 2**20),
        cost_estimate=pl.CostEstimate(flops=0, bytes_accessed=4 * 2**20, transcendentals=0),
        name="gather_rows",
    )(req, slab)


def compact_kernel(owner_ref, rank_ref, recv_ref, out_ref):
    for p in range(SEL // 2):
        a, b = 2 * p, 2 * p + 1
        out_ref[:, p * LANES : (p + 1) * LANES] = join_halves(
            recv_ref[owner_ref[a]], rank_ref[a], recv_ref[owner_ref[b]], rank_ref[b]
        )


def compact(owner, rank, recv):
    return pl.pallas_call(
        compact_kernel,
        out_shape=jax.ShapeDtypeStruct((FEAT, KEYS), jnp.bfloat16),
        in_specs=[
            pl.BlockSpec(memory_space=pltpu.SMEM),
            pl.BlockSpec(memory_space=pltpu.SMEM),
            pl.BlockSpec(memory_space=pltpu.VMEM),
        ],
        out_specs=pl.BlockSpec(memory_space=pltpu.VMEM),
        compiler_params=pltpu.CompilerParams(vmem_limit_bytes=16 * 2**20),
        cost_estimate=pl.CostEstimate(flops=0, bytes_accessed=2 * 2**20, transcendentals=0),
        name="compact",
    )(owner, rank, recv)


def attend_kernel(info_ref, pos_ref, q_ref, k0, k1, k2, k3, w_ref, out_ref, keys, sem):
    rows = q_ref.shape[0]

    @pl.when(pl.program_id(0) == 0)
    def _():
        copies = []
        for n, ref in enumerate((k0, k1, k2, k3)):
            part = lax.rem(info_ref[1] + XDIM - n, XDIM)
            place = pl.ds(pl.multiple_of(part * FEAT, 16), FEAT)
            copies.append(pltpu.make_async_copy(ref, keys.at[place, :], sem.at[n]))
        for copy in copies:
            copy.start()
        for copy in copies:
            copy.wait()

    tok = lax.broadcasted_iota(jnp.int32, (rows, 1), 0) % BLOCK
    query_pos = info_ref[0] + tok
    q = q_ref[...]
    width = 512
    scores = []
    for c in range(0, KEYS, width):
        s = jnp.dot(q, keys[:, c : c + width], preferred_element_type=jnp.float32)
        scores.append(jnp.where(pos_ref[:, c : c + width] <= query_pos, s, -jnp.inf))
    peak = jnp.max(functools.reduce(jnp.maximum, scores), axis=1, keepdims=True)
    total = jnp.zeros((rows, width), jnp.float32)
    acc = jnp.zeros((rows, LATENT), jnp.float32)
    for n, s in enumerate(scores):
        p = jnp.exp2((s - peak) * (SCALE * LOG2E))
        total = total + p
        acc = acc + lax.dot_general(
            p.astype(jnp.bfloat16),
            keys[:LATENT, n * width : (n + 1) * width],
            (((1,), (1,)), ((), ())),
            preferred_element_type=jnp.float32,
        )
    attended = (acc / jnp.sum(total, axis=1, keepdims=True)).astype(jnp.bfloat16)
    for n in range(rows // BLOCK):
        values = jnp.dot(attended[n * BLOCK : (n + 1) * BLOCK], w_ref[n], preferred_element_type=jnp.float32)
        out_ref[:, n * VHEAD : (n + 1) * VHEAD] = values.astype(jnp.bfloat16)


def attend(info, pos, q, chunks, w_uv):
    rows_all = q.shape[0]
    tile = 512
    heads = tile // BLOCK
    whole = pl.BlockSpec(memory_space=pl.ANY)
    return pl.pallas_call(
        attend_kernel,
        grid=(rows_all // tile,),
        out_shape=jax.ShapeDtypeStruct((BLOCK, rows_all // BLOCK * VHEAD), jnp.bfloat16),
        in_specs=[
            pl.BlockSpec(memory_space=pltpu.SMEM),
            pl.BlockSpec(pos.shape, lambda i: (0, 0)),
            pl.BlockSpec((tile, WIDTH), lambda i: (i, 0)),
            whole,
            whole,
            whole,
            whole,
            pl.BlockSpec((heads, LATENT, VHEAD), lambda i: (i, 0, 0)),
        ],
        out_specs=pl.BlockSpec((BLOCK, heads * VHEAD), lambda i: (0, i)),
        scratch_shapes=[pltpu.VMEM((WIDTH, KEYS), jnp.bfloat16), pltpu.SemaphoreType.DMA((XDIM,))],
        compiler_params=pltpu.CompilerParams(vmem_limit_bytes=32 * 2**20),
        cost_estimate=pl.CostEstimate(flops=5 * 10**9, bytes_accessed=8 * 2**20, transcendentals=2**21),
        name="attend",
    )(info, pos, q, *chunks, w_uv)


def project_kernel(info_ref, *refs):
    pieces = refs[: 2 * GROUP]
    w, own_ref, other_ref, rows, row_sem = refs[2 * GROUP :]
    x, y, core = info_ref[0], info_ref[1], info_ref[3]
    copies = []
    for n, ref in enumerate(pieces):
        start = n // 2 * LANES + jnp.bitwise_xor(core, n % 2) * BLOCK
        place = pl.ds(pl.multiple_of(start, BLOCK), BLOCK)
        copies.append(pltpu.make_async_copy(ref, rows.at[place, :], row_sem.at[n]))
    for copy in copies:
        copy.start()
    for copy in copies:
        copy.wait()
    half = own_ref.shape[2]
    upper = lax.shift_right_logical(y, 1)
    for j in range(2):
        for side, out_ref in enumerate((own_ref, other_ref)):
            col = pl.multiple_of((2 * j + jnp.bitwise_xor(core, side)) * half, half)
            out = jnp.dot(rows[...], w[:, pl.ds(col, half)], preferred_element_type=jnp.float32)
            out = out.astype(jnp.bfloat16)
            for n in range(GROUP):
                to = jnp.bitwise_xor(2 * upper + j, 2 * n)
                out_ref[jnp.bitwise_and(to + XDIM - x, XDIM - 1)] = out[n * LANES : (n + 1) * LANES]


def project(info, pieces, w):
    depth, cols = w.shape
    count = GROUP * LANES
    return pl.pallas_call(
        project_kernel,
        in_specs=[pl.BlockSpec(memory_space=pltpu.SMEM)]
        + [pl.BlockSpec(memory_space=pl.ANY)] * (2 * GROUP)
        + [pl.BlockSpec(memory_space=pltpu.VMEM)],
        out_specs=[pl.BlockSpec(memory_space=pltpu.VMEM)] * 2,
        out_shape=[jax.ShapeDtypeStruct((XDIM, LANES, cols // 4), jnp.bfloat16)] * 2,
        scratch_shapes=[pltpu.VMEM((count, depth), jnp.bfloat16), pltpu.SemaphoreType.DMA((2 * GROUP,))],
        compiler_params=pltpu.CompilerParams(vmem_limit_bytes=14 * 2**20),
        cost_estimate=pl.CostEstimate(flops=10**9, bytes_accessed=6 * 2**20, transcendentals=0),
        name="project",
    )(info, *pieces, w)


def assemble_kernel(info_ref, *refs):
    shards, w, sem = refs[:ZDIM], refs[ZDIM], refs[ZDIM + 1]
    copies = []
    for n, ref in enumerate(shards):
        for j in range(2):
            col = j * ZDIM * VHEAD + jnp.bitwise_and(info_ref[2] + n, ZDIM - 1) * VHEAD
            place = pl.ds(pl.multiple_of(col, VHEAD), VHEAD)
            copies.append(
                pltpu.make_async_copy(ref.at[:, pl.ds(j * VHEAD, VHEAD)], w.at[:, place], sem.at[2 * n + j])
            )
    for copy in copies:
        copy.start()
    for copy in copies:
        copy.wait()


def assemble(info, shards):
    depth, cols = shards[0].shape
    return pl.pallas_call(
        assemble_kernel,
        in_specs=[pl.BlockSpec(memory_space=pltpu.SMEM)] + [pl.BlockSpec(memory_space=pl.ANY)] * ZDIM,
        out_specs=pl.BlockSpec(memory_space=pl.ANY),
        out_shape=jax.ShapeDtypeStruct((depth, ZDIM * cols), jnp.bfloat16),
        scratch_shapes=[pltpu.SemaphoreType.DMA((2 * ZDIM,))],
        compiler_params=pltpu.CompilerParams(vmem_limit_bytes=4 * 2**20),
        cost_estimate=pl.CostEstimate(flops=0, bytes_accessed=8 * 2**20, transcendentals=0),
        name="assemble",
    )(info, *shards)


def per_device(queries, latents, selected, w_uv, w_out):
    n_ctx = lax.axis_size("ctx")
    n_head = lax.axis_size("head")
    shard = lax.axis_index("ctx")
    head = lax.axis_index("head")
    core = jnp.bitwise_and(head, 1)
    x = lax.shift_right_logical(head, 1)
    y = lax.shift_right_logical(shard, 3)
    z = jnp.bitwise_and(shard, ZDIM - 1)
    tok_dev, heads_here, width = queries.shape
    blocks_dev = latents.shape[0] // BLOCK
    first_block = blocks_dev * n_ctx - (tok_dev // BLOCK) * n_ctx
    swap = [(i, i ^ 1) for i in range(n_head)]

    def along_x(value, d):
        return lax.ppermute(value, "head", [(i, (i + 2 * d) % n_head) for i in range(n_head)])

    def along_y(value, d):
        return lax.ppermute(value, "ctx", [(i, (i + ZDIM * d) % n_ctx) for i in range(n_ctx)])

    def along_z(value, d):
        return lax.ppermute(value, "ctx", [(i, i // ZDIM * ZDIM + (i + d) % ZDIM) for i in range(n_ctx)])

    picks = jnp.where(core == 0, selected[0], selected[1])
    owner = lax.shift_right_logical(picks, 6)
    local = jnp.bitwise_and(picks, blocks_dev - 1)
    order = jnp.arange(SEL, dtype=jnp.int32)
    same = (owner[:, None] == owner[None, :]) & (order[None, :] < order[:, None])
    rank = jnp.sum(same.astype(jnp.int32), axis=1)
    slot = owner * PER_OWNER + rank
    match = slot[:, None, None] == (
        jnp.arange(n_ctx, dtype=jnp.int32)[None, :, None] * PER_OWNER
        + jnp.arange(LANES, dtype=jnp.int32)[None, None, :] // BLOCK
    )
    wanted = jnp.sum(jnp.where(match, local[:, None, None], 0), axis=0).astype(jnp.bfloat16)
    req = lax.all_to_all(wanted, "ctx", split_axis=0, concat_axis=0, tiled=True)
    req = req[:, ::BLOCK].astype(jnp.int32).reshape(-1)

    slab = lax.dynamic_slice_in_dim(latents.T, x * FEAT, FEAT, axis=0)
    up1, down1 = along_z(w_out, 1), along_z(w_out, -1)
    req, near, up1, down1 = lax.optimization_barrier((req, w_out, up1, down1))

    def peer_of(own):
        return lax.ppermute(own, "ctx", [(i, i ^ ZDIM) for i in range(n_ctx)])

    def pair(own, peer):
        even = jnp.bitwise_and(y, 1) == 0
        return jnp.where(even, jnp.concatenate([own, peer], axis=1), jnp.concatenate([peer, own], axis=1))

    piece = gather_rows(req, slab, n_ctx)
    recv = lax.all_to_all(piece, "ctx", split_axis=0, concat_axis=0, tiled=True)

    by_head = queries.transpose(1, 0, 2)
    mine = lax.dynamic_slice_in_dim(by_head, core * BLOCK, BLOCK, axis=1)
    theirs = lax.dynamic_slice_in_dim(by_head, (1 - core) * BLOCK, BLOCK, axis=1)
    got = lax.ppermute(theirs, "head", swap)
    uv_other = lax.ppermute(w_uv, "head", swap)
    q = jnp.concatenate([mine, got], axis=0).reshape(2 * heads_here * BLOCK, width)
    uv_pair = jnp.concatenate([w_uv, uv_other], axis=0)

    chunk = compact(owner, rank, recv)
    up1, down1 = pair(up1, peer_of(up1)), pair(down1, peer_of(down1))
    chunk, up1, down1 = lax.optimization_barrier((chunk, up1, down1))
    chunks = [chunk] + [along_x(chunk, d) for d in range(1, XDIM)]
    up2, down2 = along_z(up1, 1), along_z(down1, -1)
    up3, down3 = along_z(up2, 1), along_z(down2, -1)
    chunks[3], near, up3, down3 = lax.optimization_barrier((chunks[3], near, up3, down3))
    w_peer = peer_of(near)
    up4 = along_z(up3, 1)
    pos = (picks[:, None] * BLOCK + jnp.arange(BLOCK, dtype=jnp.int32)[None, :]).reshape(1, -1)
    first = (first_block + shard * (tok_dev // BLOCK) + core) * BLOCK
    values = attend(jnp.stack([first, x]), pos, q, chunks, uv_pair)

    values, w_peer = lax.optimization_barrier((values, w_peer))
    w_pair = pair(near, w_peer)
    half = heads_here * VHEAD
    own, theirs_out = values[:, :half], values[:, half:]
    swapped = lax.ppermute(theirs_out, "head", swap)
    far = [
        (c * n_head + h, (c ^ (2 * ZDIM)) * n_head + (h ^ 1)) for c in range(n_ctx) for h in range(n_head)
    ]
    pieces = [own, swapped, along_y(own, 2), lax.ppermute(theirs_out, ("ctx", "head"), far)]
    info = jnp.stack([x, y, z, core])
    kept, sent = project(info, pieces, assemble(info, [w_pair, down1, down2, down3, up4, up3, up2, up1]))
    other = lax.ppermute(sent, "head", swap)
    both = (kept.astype(jnp.float32) + other.astype(jnp.float32)).astype(jnp.bfloat16)
    total = jnp.zeros(both.shape[1:], jnp.float32)
    for d in range(XDIM):
        route = []
        for c in range(n_ctx):
            for h in range(n_head):
                to = (h + 2 * d) % n_head
                foreign = c // (2 * ZDIM) != to // 4
                route.append((c * n_head + h, (c ^ (2 * ZDIM)) * n_head + (to ^ 4) if foreign else c * n_head + to))
        total = total + lax.ppermute(both[d], ("ctx", "head"), route).astype(jnp.float32)
    return total.astype(jnp.bfloat16)


def solution(mesh):
    return jax.shard_map(
        per_device,
        mesh=mesh,
        in_specs=(
            P("ctx", "head", None),
            P("ctx", None),
            P("ctx", None),
            P("head", None, None),
            P("head", "ctx"),
        ),
        out_specs=P("ctx", "head"),
        check_vma=False,
    )
```

```python
import functools

import jax
import jax.numpy as jnp
from jax import lax
from jax.experimental import pallas as pl
from jax.experimental.pallas import tpu as pltpu
from jax.sharding import PartitionSpec as P

LATENT = 512
ROPE = 64
WIDTH = LATENT + ROPE
VHEAD = 128
BLOCK = 64
SEL = 32
KEYS = SEL * BLOCK
PER_OWNER = 2
XDIM = 4
YDIM = 4
GROUP = 2
ZDIM = 8
FEAT = WIDTH // XDIM
LANES = 2 * BLOCK
SCALE = 192.0 ** (-0.5)
LOG2E = 1.4426950408889634


def join_halves(a, a_half, b, b_half):
    lane = lax.broadcasted_iota(jnp.int32, a.shape, 1)
    low = pltpu.roll(a.astype(jnp.float32), a_half * BLOCK, 1)
    high = pltpu.roll(b.astype(jnp.float32), (1 - b_half) * BLOCK, 1)
    return jnp.where(lane < BLOCK, low, high).astype(a.dtype)


def gather_kernel(req_ref, slab_ref, out_ref):
    def pack(i, carry):
        pieces = []
        for side in range(2):
            block = req_ref[2 * i + side]
            col = pl.multiple_of(lax.shift_right_logical(block, 1) * LANES, LANES)
            pieces += [slab_ref[:, pl.ds(col, LANES)], jnp.bitwise_and(block, 1)]
        out_ref[i] = join_halves(*pieces)
        return carry

    lax.fori_loop(0, out_ref.shape[0], pack, 0, unroll=8)


def gather_rows(req, slab, n_ctx):
    return pl.pallas_call(
        gather_kernel,
        out_shape=jax.ShapeDtypeStruct((n_ctx, FEAT, LANES), jnp.bfloat16),
        in_specs=[
            pl.BlockSpec(memory_space=pltpu.SMEM),
            pl.BlockSpec(memory_space=pltpu.VMEM),
        ],
        out_specs=pl.BlockSpec(memory_space=pltpu.VMEM),
        compiler_params=pltpu.CompilerParams(vmem_limit_bytes=16 * 2**20),
        cost_estimate=pl.CostEstimate(flops=0, bytes_accessed=4 * 2**20, transcendentals=0),
        name="gather_rows",
    )(req, slab)


def compact_kernel(owner_ref, rank_ref, recv_ref, out_ref):
    for p in range(SEL // 2):
        a, b = 2 * p, 2 * p + 1
        out_ref[:, p * LANES : (p + 1) * LANES] = join_halves(
            recv_ref[owner_ref[a]], rank_ref[a], recv_ref[owner_ref[b]], rank_ref[b]
        )


def compact(owner, rank, recv):
    return pl.pallas_call(
        compact_kernel,
        out_shape=jax.ShapeDtypeStruct((FEAT, KEYS), jnp.bfloat16),
        in_specs=[
            pl.BlockSpec(memory_space=pltpu.SMEM),
            pl.BlockSpec(memory_space=pltpu.SMEM),
            pl.BlockSpec(memory_space=pltpu.VMEM),
        ],
        out_specs=pl.BlockSpec(memory_space=pltpu.VMEM),
        compiler_params=pltpu.CompilerParams(vmem_limit_bytes=16 * 2**20),
        cost_estimate=pl.CostEstimate(flops=0, bytes_accessed=2 * 2**20, transcendentals=0),
        name="compact",
    )(owner, rank, recv)


def attend_kernel(info_ref, pos_ref, q_ref, k0, k1, k2, k3, w_ref, own_ref, other_ref, keys, sem):
    rows = q_ref.shape[0]

    @pl.when(pl.program_id(0) == 0)
    def _():
        copies = []
        for n, ref in enumerate((k0, k1, k2, k3)):
            part = lax.rem(info_ref[1] + XDIM - n, XDIM)
            place = pl.ds(pl.multiple_of(part * FEAT, 16), FEAT)
            copies.append(pltpu.make_async_copy(ref, keys.at[place, :], sem.at[n]))
        for copy in copies:
            copy.start()
        for copy in copies:
            copy.wait()

    tok = lax.broadcasted_iota(jnp.int32, (rows, 1), 0) % BLOCK
    query_pos = info_ref[0] + tok
    q = q_ref[...]
    width = 512
    scores = []
    for c in range(0, KEYS, width):
        s = jnp.dot(q, keys[:, c : c + width], preferred_element_type=jnp.float32)
        scores.append(jnp.where(pos_ref[:, c : c + width] <= query_pos, s, -jnp.inf))
    peak = jnp.max(functools.reduce(jnp.maximum, scores), axis=1, keepdims=True)
    total = jnp.zeros((rows, width), jnp.float32)
    acc = jnp.zeros((rows, LATENT), jnp.float32)
    for n, s in enumerate(scores):
        p = jnp.exp2((s - peak) * (SCALE * LOG2E))
        total = total + p
        acc = acc + lax.dot_general(
            p.astype(jnp.bfloat16),
            keys[:LATENT, n * width : (n + 1) * width],
            (((1,), (1,)), ((), ())),
            preferred_element_type=jnp.float32,
        )
    attended = (acc / jnp.sum(total, axis=1, keepdims=True)).astype(jnp.bfloat16)
    parts = [
        jnp.dot(attended[n * BLOCK : (n + 1) * BLOCK], w_ref[n], preferred_element_type=jnp.float32).astype(jnp.bfloat16)
        for n in range(rows // BLOCK)
    ]
    for step, out_ref in enumerate((own_ref, other_ref)):

        @pl.when(pl.program_id(0) == step)
        def _():
            for n, part in enumerate(parts):
                out_ref[:, n * VHEAD : (n + 1) * VHEAD] = part


def attend(info, pos, q, chunks, w_uv):
    rows_all = q.shape[0]
    tile = 512
    heads = tile // BLOCK
    whole = pl.BlockSpec(memory_space=pl.ANY)
    return pl.pallas_call(
        attend_kernel,
        grid=(rows_all // tile,),
        out_shape=[jax.ShapeDtypeStruct((BLOCK, heads * VHEAD), jnp.bfloat16)] * 2,
        in_specs=[
            pl.BlockSpec(memory_space=pltpu.SMEM),
            pl.BlockSpec(pos.shape, lambda i: (0, 0)),
            pl.BlockSpec((tile, WIDTH), lambda i: (i, 0)),
            whole,
            whole,
            whole,
            whole,
            pl.BlockSpec((heads, LATENT, VHEAD), lambda i: (i, 0, 0)),
        ],
        out_specs=[pl.BlockSpec((BLOCK, heads * VHEAD), lambda i: (0, 0))] * 2,
        scratch_shapes=[pltpu.VMEM((WIDTH, KEYS), jnp.bfloat16), pltpu.SemaphoreType.DMA((XDIM,))],
        compiler_params=pltpu.CompilerParams(vmem_limit_bytes=32 * 2**20),
        cost_estimate=pl.CostEstimate(flops=5 * 10**9, bytes_accessed=8 * 2**20, transcendentals=2**21),
        name="attend",
    )(info, pos, q, *chunks, w_uv)


def project_kernel(info_ref, *refs):
    pieces = refs[: 2 * GROUP]
    w, own_ref, other_ref, rows, row_sem = refs[2 * GROUP :]
    x, y, core = info_ref[0], info_ref[1], info_ref[3]
    copies = []
    for n, ref in enumerate(pieces):
        start = n // 2 * LANES + jnp.bitwise_xor(core, n % 2) * BLOCK
        place = pl.ds(pl.multiple_of(start, BLOCK), BLOCK)
        copies.append(pltpu.make_async_copy(ref, rows.at[place, :], row_sem.at[n]))
    for copy in copies:
        copy.start()
    for copy in copies:
        copy.wait()
    half = own_ref.shape[2]
    upper = lax.shift_right_logical(y, 1)
    for j in range(2):
        for side, out_ref in enumerate((own_ref, other_ref)):
            col = pl.multiple_of((2 * j + jnp.bitwise_xor(core, side)) * half, half)
            out = jnp.dot(rows[...], w[:, pl.ds(col, half)], preferred_element_type=jnp.float32)
            out = out.astype(jnp.bfloat16)
            for n in range(GROUP):
                to = jnp.bitwise_xor(2 * upper + j, 2 * n)
                out_ref[jnp.bitwise_and(to + XDIM - x, XDIM - 1)] = out[n * LANES : (n + 1) * LANES]


def project(info, pieces, w):
    depth, cols = w.shape
    count = GROUP * LANES
    return pl.pallas_call(
        project_kernel,
        in_specs=[pl.BlockSpec(memory_space=pltpu.SMEM)]
        + [pl.BlockSpec(memory_space=pl.ANY)] * (2 * GROUP)
        + [pl.BlockSpec(memory_space=pltpu.VMEM)],
        out_specs=[pl.BlockSpec(memory_space=pltpu.VMEM)] * 2,
        out_shape=[jax.ShapeDtypeStruct((XDIM, LANES, cols // 4), jnp.bfloat16)] * 2,
        scratch_shapes=[pltpu.VMEM((count, depth), jnp.bfloat16), pltpu.SemaphoreType.DMA((2 * GROUP,))],
        compiler_params=pltpu.CompilerParams(vmem_limit_bytes=14 * 2**20),
        cost_estimate=pl.CostEstimate(flops=10**9, bytes_accessed=6 * 2**20, transcendentals=0),
        name="project",
    )(info, *pieces, w)


def assemble_kernel(info_ref, *refs):
    shards, w, sem = refs[:ZDIM], refs[ZDIM], refs[ZDIM + 1]
    copies = []
    for n, ref in enumerate(shards):
        for j in range(2):
            col = j * ZDIM * VHEAD + jnp.bitwise_and(info_ref[2] + n, ZDIM - 1) * VHEAD
            place = pl.ds(pl.multiple_of(col, VHEAD), VHEAD)
            copies.append(
                pltpu.make_async_copy(ref.at[:, pl.ds(j * VHEAD, VHEAD)], w.at[:, place], sem.at[2 * n + j])
            )
    for copy in copies:
        copy.start()
    for copy in copies:
        copy.wait()


def assemble(info, shards):
    depth, cols = shards[0].shape
    return pl.pallas_call(
        assemble_kernel,
        in_specs=[pl.BlockSpec(memory_space=pltpu.SMEM)] + [pl.BlockSpec(memory_space=pl.ANY)] * ZDIM,
        out_specs=pl.BlockSpec(memory_space=pl.ANY),
        out_shape=jax.ShapeDtypeStruct((depth, ZDIM * cols), jnp.bfloat16),
        scratch_shapes=[pltpu.SemaphoreType.DMA((2 * ZDIM,))],
        compiler_params=pltpu.CompilerParams(vmem_limit_bytes=4 * 2**20),
        cost_estimate=pl.CostEstimate(flops=0, bytes_accessed=8 * 2**20, transcendentals=0),
        name="assemble",
    )(info, *shards)


def per_device(queries, latents, selected, w_uv, w_out):
    n_ctx = lax.axis_size("ctx")
    n_head = lax.axis_size("head")
    shard = lax.axis_index("ctx")
    head = lax.axis_index("head")
    core = jnp.bitwise_and(head, 1)
    x = lax.shift_right_logical(head, 1)
    y = lax.shift_right_logical(shard, 3)
    z = jnp.bitwise_and(shard, ZDIM - 1)
    tok_dev, heads_here, width = queries.shape
    blocks_dev = latents.shape[0] // BLOCK
    first_block = blocks_dev * n_ctx - (tok_dev // BLOCK) * n_ctx
    swap = [(i, i ^ 1) for i in range(n_head)]

    def along_x(value, d):
        return lax.ppermute(value, "head", [(i, (i + 2 * d) % n_head) for i in range(n_head)])

    def along_y(value, d):
        return lax.ppermute(value, "ctx", [(i, (i + ZDIM * d) % n_ctx) for i in range(n_ctx)])

    def along_z(value, d):
        return lax.ppermute(value, "ctx", [(i, i // ZDIM * ZDIM + (i + d) % ZDIM) for i in range(n_ctx)])

    picks = jnp.where(core == 0, selected[0], selected[1])
    owner = lax.shift_right_logical(picks, 6)
    local = jnp.bitwise_and(picks, blocks_dev - 1)
    order = jnp.arange(SEL, dtype=jnp.int32)
    same = (owner[:, None] == owner[None, :]) & (order[None, :] < order[:, None])
    rank = jnp.sum(same.astype(jnp.int32), axis=1)
    slot = owner * PER_OWNER + rank
    match = slot[:, None, None] == (
        jnp.arange(n_ctx, dtype=jnp.int32)[None, :, None] * PER_OWNER
        + jnp.arange(LANES, dtype=jnp.int32)[None, None, :] // BLOCK
    )
    wanted = jnp.sum(jnp.where(match, local[:, None, None], 0), axis=0).astype(jnp.bfloat16)
    req = lax.all_to_all(wanted, "ctx", split_axis=0, concat_axis=0, tiled=True)
    req = req[:, ::BLOCK].astype(jnp.int32).reshape(-1)

    slab = lax.dynamic_slice_in_dim(latents.T, x * FEAT, FEAT, axis=0)
    up1, down1 = along_z(w_out, 1), along_z(w_out, -1)
    req, near, up1, down1 = lax.optimization_barrier((req, w_out, up1, down1))

    def peer_of(own):
        return lax.ppermute(own, "ctx", [(i, i ^ ZDIM) for i in range(n_ctx)])

    def pair(own, peer):
        even = jnp.bitwise_and(y, 1) == 0
        return jnp.where(even, jnp.concatenate([own, peer], axis=1), jnp.concatenate([peer, own], axis=1))

    piece = gather_rows(req, slab, n_ctx)
    recv = lax.all_to_all(piece, "ctx", split_axis=0, concat_axis=0, tiled=True)

    by_head = queries.transpose(1, 0, 2)
    mine = lax.dynamic_slice_in_dim(by_head, core * BLOCK, BLOCK, axis=1)
    theirs = lax.dynamic_slice_in_dim(by_head, (1 - core) * BLOCK, BLOCK, axis=1)
    got = lax.ppermute(theirs, "head", swap)
    uv_other = lax.ppermute(w_uv, "head", swap)
    q = jnp.concatenate([mine, got], axis=0).reshape(2 * heads_here * BLOCK, width)
    uv_pair = jnp.concatenate([w_uv, uv_other], axis=0)

    chunk = compact(owner, rank, recv)
    up1, down1 = pair(up1, peer_of(up1)), pair(down1, peer_of(down1))
    chunk, up1, down1 = lax.optimization_barrier((chunk, up1, down1))
    chunks = [chunk] + [along_x(chunk, d) for d in range(1, XDIM)]
    up2, down2 = along_z(up1, 1), along_z(down1, -1)
    up3, down3 = along_z(up2, 1), along_z(down2, -1)
    chunks[3], near, up3, down3 = lax.optimization_barrier((chunks[3], near, up3, down3))
    w_peer = peer_of(near)
    up4 = along_z(up3, 1)
    pos = (picks[:, None] * BLOCK + jnp.arange(BLOCK, dtype=jnp.int32)[None, :]).reshape(1, -1)
    first = (first_block + shard * (tok_dev // BLOCK) + core) * BLOCK
    own, theirs_out = attend(jnp.stack([first, x]), pos, q, chunks, uv_pair)

    own, theirs_out, w_peer = lax.optimization_barrier((own, theirs_out, w_peer))
    w_pair = pair(near, w_peer)
    swapped = lax.ppermute(theirs_out, "head", swap)
    far = [
        (c * n_head + h, (c ^ (2 * ZDIM)) * n_head + (h ^ 1)) for c in range(n_ctx) for h in range(n_head)
    ]
    pieces = [own, swapped, along_y(own, 2), lax.ppermute(theirs_out, ("ctx", "head"), far)]
    info = jnp.stack([x, y, z, core])
    kept, sent = project(info, pieces, assemble(info, [w_pair, down1, down2, down3, up4, up3, up2, up1]))
    other = lax.ppermute(sent, "head", swap)
    both = (kept.astype(jnp.float32) + other.astype(jnp.float32)).astype(jnp.bfloat16)
    total = jnp.zeros(both.shape[1:], jnp.float32)
    for d in range(XDIM):
        route = []
        for c in range(n_ctx):
            for h in range(n_head):
                to = (h + 2 * d) % n_head
                foreign = c // (2 * ZDIM) != to // 4
                route.append((c * n_head + h, (c ^ (2 * ZDIM)) * n_head + (to ^ 4) if foreign else c * n_head + to))
        total = total + lax.ppermute(both[d], ("ctx", "head"), route).astype(jnp.float32)
    return total.astype(jnp.bfloat16)


def solution(mesh):
    return jax.shard_map(
        per_device,
        mesh=mesh,
        in_specs=(
            P("ctx", "head", None),
            P("ctx", None),
            P("ctx", None),
            P("head", None, None),
            P("head", "ctx"),
        ),
        out_specs=P("ctx", "head"),
        check_vma=False,
    )
```
